32 devices in a mesh: groups: 1, mode: 32 (over z, y, x, core).
Axes of the slice: x: 2, y: 2, z: 4, core: 2. Of those that a mesh axis runs over, the one named last changes fastest.
Arguments:
- basis: bfloat16 [384, 16384], P('groups', 'mode')
- slab_region: int32 [128], P(('groups', 'mode')), may hold values from 0 to 8
- coef_index: int32 [9, 6], P('groups'), may hold values from 0 to 8
- coef_table: float32 [8], P('groups'), may hold values from 0.2 to 5
Outputs:
- gram: float32 [21, 384, 384], P(None, ('groups', 'mode'))
The draws below stay inside these ranges and needn't reach their ends.
All inputs are finite; a program needn't handle non-finite values.
Results may differ from the reference program's by a relative error of at most 0.0005.
The reference program's roundings to bfloat16 on the way (of `actions`) count: a program that leaves them out, or rounds other values in their place, can miss the bound.
Values may be sent and summed in bfloat16 or wider, within the bound.
A program may use at most 128 MiB of HBM per device.

```python
import math
import jax
import jax.numpy as jnp
from jax import lax

NB = 384
SLABW = 128
REGIONS = 9
TERMS = 6
NCOEF = 8
SLABS = 128
CELLS = 16384
N_MODE = 32


def draw_basis(key, part):
    key_mode = jax.random.fold_in(jax.random.fold_in(key, 17), 0)
    key_cell = jax.random.fold_in(jax.random.fold_in(key, 17), 1)
    key_main = jax.random.fold_in(jax.random.fold_in(key, 17), 2)
    key_pair = jax.random.fold_in(jax.random.fold_in(key, 17), 4)
    mode_scale = jnp.exp(math.log(10.0) * jax.random.uniform(key_mode, (NB,), jnp.float32) - math.log(10.0) * 0.5)
    ramp = jnp.arange(CELLS, dtype=jnp.float32) / CELLS
    cell_scale = jnp.exp(math.log(3.0) * ramp + math.log(3.0) * jax.random.uniform(key_cell, (CELLS,), jnp.float32))
    cell_block = jnp.arange(CELLS, dtype=jnp.int32) // (CELLS // N_MODE)
    mode_block = jnp.arange(NB, dtype=jnp.int32) // (NB // N_MODE)
    pairing = jax.random.permutation(key_pair, N_MODE)
    boost = jnp.where(pairing[cell_block][None, :] == mode_block[:, None], 4.0, 1.0)
    values = jnp.clip(jax.random.normal(key_main, (NB, CELLS), jnp.float32), -6.0, 6.0)
    return (boost * mode_scale[:, None] * cell_scale[None, :] * values).astype(jnp.bfloat16)


def touch_ends(values, rng, least, largest):
    longest = values.shape.index(max(values.shape))
    spots = []
    for shift in (0, 1):
        where = [jax.random.randint(jax.random.fold_in(rng, axis), (), 0, length) for axis, length in enumerate(values.shape)]
        where[longest] = (where[longest] + shift) % values.shape[longest]
        spots.append(tuple(where))
    return values.at[spots[0]].set(least).at[spots[1]].set(largest)


def setup_inputs(seed: int = 0, part: int = 0) -> dict:
    arg_keys = jax.random.split(jax.random.key(seed), 5)
    own_keys = jax.random.split(jax.random.fold_in(arg_keys[4], part), 5)
    basis = draw_basis(jax.random.fold_in(jax.random.fold_in(arg_keys[4], part), 71), part)
    slab_region = touch_ends(jax.random.randint(own_keys[1], (SLABS,), 0, REGIONS), jax.random.fold_in(own_keys[1], 1), 0, REGIONS - 1).astype(jnp.int32)
    coef_index = touch_ends(jax.random.randint(own_keys[2], (REGIONS, TERMS), 0, NCOEF + 1), jax.random.fold_in(own_keys[2], 1), 0, NCOEF).astype(jnp.int32)
    coef_table = jnp.clip(jnp.exp(jax.random.uniform(own_keys[3], (NCOEF,), jnp.float32, math.log(0.2), math.log(5.0))), 0.2, 5.0)
    return {"basis": basis, "slab_region": slab_region, "coef_index": coef_index, "coef_table": coef_table}


def slab_weights(slab_region, coef_index, coef_table):
    table_hit = (coef_index[:, :, None] == jnp.arange(NCOEF, dtype=jnp.int32)[None, None, :]).astype(jnp.float32)
    kappa = lax.optimization_barrier(jnp.sum(table_hit * coef_table[None, None, :], axis=2))
    region_hit = (slab_region[:, None] == jnp.arange(REGIONS, dtype=jnp.int32)[None, :]).astype(jnp.float32)
    return lax.optimization_barrier(jnp.sum(region_hit[:, :, None] * kappa[None, :, :], axis=1))

def one_action(field, weight, term):
    rows = field.shape[0]
    if term == 0:
        stencil = 2.0 * field - jnp.roll(field, 1, axis=1) - jnp.roll(field, -1, axis=1)
    elif term == 1:
        zero_col = jnp.zeros((rows, SLABS, 1), jnp.float32)
        left_w = jnp.concatenate([zero_col, field[:, :, :-1]], axis=2)
        right_w = jnp.concatenate([field[:, :, 1:], zero_col], axis=2)
        stencil = 2.0 * field - left_w - right_w
    elif term == 2:
        stencil = field - jnp.roll(field, 1, axis=1)
    elif term == 3:
        stencil = field - jnp.roll(field, -1, axis=1)
    elif term == 4:
        stencil = field - field[:, :, ::-1]
    else:
        stencil = field
    return (weight[None, :, None] * stencil).reshape(rows, SLABS * SLABW).astype(jnp.bfloat16)

def reference(basis, slab_region, coef_index, coef_table):
    slab_kappa = slab_weights(slab_region, coef_index, coef_table)
    field = basis.astype(jnp.float32).reshape(NB, SLABS, SLABW)
    actions = [one_action(field, slab_kappa[:, term], term) for term in range(TERMS)]
    sums = []
    for term in range(TERMS):
        values = actions[term].astype(jnp.float32)
        sums.append(jnp.sum(values * values))
    level = jnp.stack(sums) / (NB * CELLS) + 1e-06
    blocks = []
    for first in range(TERMS):
        for second in range(first, TERMS):
            raw = jnp.dot(actions[first], actions[second].T, preferred_element_type=jnp.float32)
            blocks.append(raw / (CELLS * jnp.sqrt(level[first] * level[second])))
    return jnp.stack(blocks, axis=0)
```

```python
import functools

import jax
import jax.numpy as jnp
from jax import lax
from jax.experimental import pallas as pl
from jax.experimental.pallas import tpu as pltpu
from jax.sharding import PartitionSpec as P

MEMBERS = 4
CHUNK = 3


def near_size(outer):
    size = 1
    while outer % (2 * size) == 0 and 8 * size * size <= outer:
        size *= 2
    return size


def chunk_list(terms):
    chunks = []
    for second in reversed(range(terms)):
        pieces = -(-(second + 1) // CHUNK)
        first = 0
        for piece in range(pieces):
            count = -(-(second + 1 - first) // (pieces - piece))
            chunks.append((second, first, count))
            first += count
    return chunks


def one_action(term, here, before, after, across, opposite, kappa):
    value = here.astype(jnp.float32)
    if term == 0:
        stencil = 2.0 * value - before.astype(jnp.float32) - after.astype(jnp.float32)
    elif term == 1:
        stencil = jnp.dot(here, across, preferred_element_type=jnp.float32)
    elif term == 2:
        stencil = value - before.astype(jnp.float32)
    elif term == 3:
        stencil = value - after.astype(jnp.float32)
    elif term == 4:
        stencil = jnp.dot(here, opposite, preferred_element_type=jnp.float32)
    else:
        stencil = value
    return (kappa * stencil).astype(jnp.bfloat16)


def coded(value, floor=1e-30):
    peak = jnp.maximum(jnp.max(jnp.abs(value), axis=0, keepdims=True), floor)
    return jnp.round(value * (32000.0 / peak)), peak * (1.0 / 32000.0)


def gram_kernel(terms, near, far, own, slabs_dev, total_cells, *refs):
    basis, region, index, table, out = refs[:5]
    chunks = chunk_list(terms)
    count = len(chunks)
    field, weights, mine, pickf, lhs1, lhs2, act1, act2, whole = refs[5:14]
    at = 14
    acc = refs[at : at + terms]
    at += terms
    buffers = []
    for _ in range(9):
        buffers.append(refs[at : at + count])
        at += count
    codes1, got1, scale1, gots1, codes2, got2, scale2, gots2, keep = buffers
    lvl0, lvl1, lvl2, in0, in1, in2 = refs[at : at + 6]
    at += 6
    (load_sem, xs, xr, sib_s, sib_r, rel_s, rel_r, hs, hr, hrel_s, hrel_r, ks, kr) = refs[at : at + 13]
    at += 13
    cs1, cr1, ss1, sr1, cs2, cr2, ss2, sr2, ls0, lr0, ls1, lr1, ls2, lr2 = refs[at:]

    rows, width = field.shape[1], field.shape[2]
    entries = table.shape[0]
    slabs = MEMBERS * slabs_dev
    outer = near * far
    local = outer * own
    share = far * own
    me = lax.axis_index("mode")
    group = me // MEMBERS
    member = me % MEMBERS
    chip = member // 2
    core = member % 2
    a = lax.rem(group, near)
    b = group // near

    sibling = group * MEMBERS + chip * 2 + 1 - core
    partner_member = (1 - chip) * 2 + core
    partner = group * MEMBERS + partner_member

    def member_peer(d):
        return group * MEMBERS + lax.rem(member + d, MEMBERS)

    def near_peer(d):
        return (b * near + lax.rem(a + d, near)) * MEMBERS + member

    def far_peer(d):
        return (lax.rem(b + d, far) * near + a) * MEMBERS + member

    def group_peer(d):
        return lax.rem(group + d, outer) * MEMBERS + member

    def remote(src, dst, send, recv, peer):
        return pltpu.make_async_remote_copy(
            src_ref=src,
            dst_ref=dst,
            send_sem=send,
            recv_sem=recv,
            device_id={"mode": peer},
            device_id_type=pl.DeviceIdType.MESH,
        )

    first_slot = 1 + member * slabs_dev
    loads = [
        pltpu.make_async_copy(
            basis.at[:, pl.ds(s * width, width)], field.at[first_slot + s], load_sem.at[s]
        )
        for s in range(slabs_dev)
    ]
    for copy in loads:
        copy.start()

    barrier = pltpu.get_barrier_semaphore()
    greeted = [member_peer(d) for d in range(1, MEMBERS)]
    greeted += [near_peer(d) for d in range(1, near)]
    greeted += [far_peer(d) for d in range(1, far)]
    greeted += [group_peer(1), group_peer(outer - 1)]
    for peer in greeted:
        pl.semaphore_signal(
            barrier, inc=1, device_id={"mode": peer}, device_id_type=pl.DeviceIdType.MESH
        )
    pl.semaphore_wait(barrier, len(greeted))
    for copy in loads:
        copy.wait()

    def turn(k):
        return k + core * (slabs_dev - 1 - 2 * k)

    across_copies = []
    relays = []
    for k in range(slabs_dev):
        slot = first_slot + turn(k)
        across_copies.append(
            remote(field.at[slot], field.at[slot], xs.at[k], xr.at[k], partner)
        )
        slot = 1 + partner_member * slabs_dev + turn(k)
        relays.append(
            remote(field.at[slot], field.at[slot], rel_s.at[k], rel_r.at[k], sibling)
        )
    span = pl.ds(first_slot, slabs_dev)
    beside = remote(field.at[span], field.at[span], sib_s.at[0], sib_r.at[0], sibling)
    for copy in across_copies:
        copy.start()
    beside.start()
    edge = 1 + core * (slabs - 1)
    beyond = (1 - core) * (slabs + 1)
    halo = remote(
        field.at[edge],
        field.at[beyond],
        hs.at[0],
        hr.at[0],
        lax.rem(group + outer + 2 * core - 1, outer) * MEMBERS + member,
    )
    halo_relay = remote(field.at[beyond], field.at[beyond], hrel_s.at[0], hrel_r.at[0], sibling)

    tall = weights.shape[1]
    row_at = lax.broadcasted_iota(jnp.int32, (tall, width), 0)
    for s in range(slabs_dev):
        where = region[s]
        value = jnp.zeros((tall, width), jnp.float32)
        for term in range(terms):
            entry = index[where, term]
            kappa = jnp.where(entry < entries, table[jnp.minimum(entry, entries - 1)], 0.0)
            value = jnp.where(row_at == term, kappa, value)
        weights[member * slabs_dev + s] = value
    spot = pl.ds(member * slabs_dev, slabs_dev)
    small = [
        remote(weights.at[spot], weights.at[spot], ks.at[d - 1], kr.at[d - 1], member_peer(d))
        for d in range(1, MEMBERS)
    ]
    for copy in small:
        copy.start()

    wi = lax.broadcasted_iota(jnp.int32, (width, width), 0)
    wj = lax.broadcasted_iota(jnp.int32, (width, width), 1)
    beside_one = jnp.where((wi == wj + 1) | (wj == wi + 1), 1.0, 0.0)
    same = jnp.where(wi == wj, 1.0, 0.0)
    flip = jnp.where(wi + wj == width - 1, 1.0, 0.0)
    across = (2.0 * same - beside_one).astype(jnp.bfloat16)
    opposite = (same - flip).astype(jnp.bfloat16)
    ri = lax.broadcasted_iota(jnp.int32, (local, rows), 0)
    rj = lax.broadcasted_iota(jnp.int32, (local, rows), 1)
    source = ri
    for da in range(near):
        for db in range(far):
            place = da * far + db
            home = lax.rem(b + db, far) * near + lax.rem(a + da, near)
            shift = (home * MEMBERS + member) * own - place * own
            source = jnp.where(ri >= place * own, ri + shift, source)
    pickf[...] = jnp.where(rj == source, 1.0, 0.0)
    select = pickf[...].astype(jnp.bfloat16)

    def pick(first, number):
        for s in range(number):
            mine[first + s] = jnp.dot(
                select, field[first + s], preferred_element_type=jnp.float32
            ).astype(jnp.bfloat16)

    def acted(term, source_ref, slab):
        alone = term in (1, 4, 5)
        return one_action(
            term,
            source_ref[slab + 1],
            None if alone else source_ref[slab],
            None if alone else source_ref[slab + 2],
            across,
            opposite,
            weights[slab, term : term + 1, :],
        )

    inner_count = 2 * slabs_dev - 2
    inner_first = 2 + inner_count * chip
    part1 = [inner_first + s for s in range(inner_count)]
    part2 = [chip * (slabs - 2) + s for s in range(2)]
    part2 += [(1 - chip) * 2 * slabs_dev + s for s in range(2 * slabs_dev)]

    def own_actions(lhs, part):
        for term in range(terms):
            for s, slab in enumerate(part):
                lhs[term * local : (term + 1) * local, s * width : (s + 1) * width] = acted(
                    term, mine, slab
                )

    def all_actions(act, part, second):
        for s, slab in enumerate(part):
            act[second % 2, :, s * width : (s + 1) * width] = acted(second, field, slab)

    def product(lhs, act, second):
        return lax.dot_general(
            lhs[0 : (second + 1) * local, :],
            act[second % 2],
            (((1,), (1,)), ((), ())),
            preferred_element_type=jnp.float32,
        )

    across_copies[0].wait_recv()
    relays[0].start()
    halo.start()
    beside.wait()
    for copy in small:
        copy.wait()
    relays[0].wait_recv()
    pick(inner_first, inner_count + 2)
    own_actions(lhs1, part1)
    order = list(reversed(range(terms)))
    for spot_at, second in enumerate(order):
        all_actions(act1, part1, second)
        acc[second][...] = product(lhs1, act1, second)
        if 1 <= spot_at + 1 < slabs_dev:
            across_copies[spot_at + 1].wait_recv()
            relays[spot_at + 1].start()
        if spot_at == 2:
            halo.wait_recv()
            halo_relay.start()
    for copy in relays[1:]:
        copy.wait_recv()
    halo_relay.wait_recv()
    pick(chip * slabs, 2)
    pick((1 - chip) * (2 * slabs_dev + 2), 2 * slabs_dev)
    own_actions(lhs2, part2)

    lvl0[...] = jnp.zeros_like(lvl0)
    sends = []
    stage1 = [[] for _ in chunks]
    for second in order:
        all_actions(act2, part2, second)
        acc[second][...] += product(lhs2, act2, second)
        for n, (chunk_second, first, number) in enumerate(chunks):
            if chunk_second != second:
                continue
            for d in range(1, near):
                for i in range(number):
                    base = (first + i) * local + d * share
                    code, scale = coded(acc[second][base : base + share, :])
                    codes1[n][d - 1, i * share : (i + 1) * share, :] = code.astype(
                        jnp.int32
                    ).astype(jnp.int16)
                    scale1[n][d - 1, i : i + 1, :] = scale
                sem = n * (near - 1) + d - 1
                for src, dst, s_sem, r_sem in (
                    (scale1, gots1, ss1, sr1),
                    (codes1, got1, cs1, cr1),
                ):
                    copy = remote(
                        src[n].at[d - 1],
                        dst[n].at[d - 1],
                        s_sem.at[sem],
                        r_sem.at[sem],
                        near_peer(d),
                    )
                    copy.start()
                    stage1[n].append(copy)
                    sends.append(copy)
        lvl0[second : second + 1, :] = jnp.sum(
            acc[second][second * local : (second + 1) * local, :] * pickf[...],
            axis=0,
            keepdims=True,
        )

    def spread(src, dst, s_sem, r_sem, peer_of, number):
        copies = [
            remote(src, dst.at[d - 1], s_sem.at[d - 1], r_sem.at[d - 1], peer_of(d))
            for d in range(1, number)
        ]
        for copy in copies:
            copy.start()
        return copies

    def gathered(copies, src, dst):
        for copy in copies:
            copy.wait_recv()
        sends.extend(copies)
        total = src[...]
        for n in range(len(copies)):
            total = total + dst[n]
        return total

    level_copies = spread(lvl0, in0, ls0, lr0, near_peer, near)

    stage2 = [[] for _ in chunks]
    for n, (second, first, number) in enumerate(chunks):
        for copy in stage1[n]:
            copy.wait_recv()
        for i in range(number):
            base = (first + i) * local
            value = acc[second][base : base + share, :]
            for d in range(1, near):
                part = got1[n][d - 1, i * share : (i + 1) * share, :]
                value = value + (
                    part.astype(jnp.int32).astype(jnp.float32) * gots1[n][d - 1, i : i + 1, :]
                )
            keep[n][i * own : (i + 1) * own, :] = value[0:own]
            code, scale = coded(value[own:])
            scale2[n][i : i + 1, :] = scale
            for d in range(1, far):
                whole[d - 1, i * own : (i + 1) * own, :] = code[(d - 1) * own : d * own]
        for d in range(1, far):
            codes2[n][d - 1] = (
                whole[d - 1, 0 : number * own, :].astype(jnp.int32).astype(jnp.int16)
            )
            sem = n * (far - 1) + d - 1
            for src, dst, s_sem, r_sem in (
                (scale2[n], gots2, ss2, sr2),
                (codes2[n].at[d - 1], got2, cs2, cr2),
            ):
                copy = remote(src, dst[n].at[d - 1], s_sem.at[sem], r_sem.at[sem], far_peer(d))
                copy.start()
                stage2[n].append(copy)
                sends.append(copy)
        if n == 0:
            lvl1[...] = gathered(level_copies, lvl0, in0)
            level_copies = spread(lvl1, in1, ls1, lr1, far_peer, far)
        if n == count // 2:
            lvl2[...] = gathered(level_copies, lvl1, in1)
            level_copies = spread(lvl2, in2, ls2, lr2, member_peer, MEMBERS)

    total = gathered(level_copies, lvl2, in2)
    level = jnp.sum(total, axis=1, keepdims=True) / (rows * total_cells) + 1e-06
    for n, (second, first, number) in enumerate(chunks):
        for copy in stage2[n]:
            copy.wait_recv()
        opened = [got2[n][d - 1].astype(jnp.int32).astype(jnp.float32) for d in range(1, far)]
        for i in range(number):
            q = first + i
            value = keep[n][i * own : (i + 1) * own, :]
            for d in range(1, far):
                value = value + (
                    opened[d - 1][i * own : (i + 1) * own, :] * gots2[n][d - 1, i : i + 1, :]
                )
            factor = 1.0 / (total_cells * jnp.sqrt(level[q : q + 1] * level[second : second + 1]))
            pair = q * terms - q * (q - 1) // 2 + second - q
            out[pair] = value * factor
    for copy in sends + across_copies + relays + [halo, halo_relay]:
        copy.wait_send()


def per_device(basis, slab_region, coef_index, coef_table):
    terms = coef_index.shape[1]
    rows, cells_dev = basis.shape
    slabs_dev = slab_region.shape[0]
    width = cells_dev // slabs_dev
    devices = lax.axis_size("mode")
    outer = devices // MEMBERS
    near = near_size(outer)
    far = outer // near
    own = rows // devices
    slabs = slabs_dev * MEMBERS
    local = outer * own
    share = far * own
    chunks = chunk_list(terms)
    count = len(chunks)
    tall = terms + -terms % 8
    f32, b16, i16 = jnp.float32, jnp.bfloat16, jnp.int16
    k1 = (2 * slabs_dev - 2) * width
    k2 = (2 * slabs_dev + 2) * width
    dma = pltpu.SemaphoreType.DMA
    vmem = pltpu.VMEM
    most = max(number for _, _, number in chunks)
    scratch = [
        vmem((slabs + 2, rows, width), b16),
        vmem((slabs, tall, width), f32),
        vmem((slabs + 2, local, width), b16),
        vmem((local, rows), f32),
        vmem((terms * local, k1), b16),
        vmem((terms * local, k2), b16),
        vmem((2, rows, k1), b16),
        vmem((2, rows, k2), b16),
        vmem((far - 1, most * own, rows), f32),
    ]
    scratch += [vmem(((q + 1) * local, rows), f32) for q in range(terms)]
    scratch += [vmem((near - 1, n * share, rows), i16) for _, _, n in chunks] * 2
    scratch += [vmem((near - 1, n, rows), f32) for _, _, n in chunks] * 2
    scratch += [vmem((far - 1, n * own, rows), i16) for _, _, n in chunks] * 2
    scratch += [vmem((n, rows), f32) for _, _, n in chunks]
    scratch += [vmem((far - 1, n, rows), f32) for _, _, n in chunks]
    scratch += [vmem((n * own, rows), f32) for _, _, n in chunks]
    scratch += [vmem((tall, rows), f32)] * 3
    scratch += [vmem((n - 1, tall, rows), f32) for n in (near, far, MEMBERS)]
    scratch += [dma((slabs_dev,))] * 3
    scratch += [dma((1,))] * 2
    scratch += [dma((slabs_dev,))] * 2
    scratch += [dma((1,))] * 4
    scratch += [dma((MEMBERS - 1,))] * 2
    scratch += [dma((count * (near - 1),))] * 4
    scratch += [dma((count * (far - 1),))] * 4
    for n in (near, far, MEMBERS):
        scratch += [dma((n - 1,))] * 2
    smem = pl.BlockSpec(memory_space=pltpu.SMEM)
    return pl.pallas_call(
        functools.partial(
            gram_kernel, terms, near, far, own, slabs_dev, cells_dev * devices
        ),
        out_shape=jax.ShapeDtypeStruct((terms * (terms + 1) // 2, own, rows), f32),
        in_specs=[pl.BlockSpec(memory_space=pl.ANY), smem, smem, smem],
        out_specs=pl.BlockSpec(memory_space=pltpu.VMEM),
        scratch_shapes=scratch,
        compiler_params=pltpu.CompilerParams(
            collective_id=0, has_side_effects=True, vmem_limit_bytes=48 << 20
        ),
    )(basis, slab_region, coef_index, coef_table)


def solution(mesh):
    return jax.shard_map(
        per_device,
        mesh=mesh,
        in_specs=(P("groups", "mode"), P(("groups", "mode")), P("groups", None), P("groups")),
        out_specs=P(None, ("groups", "mode"), None),
        check_vma=False,
    )
```

```python
import functools

import jax
import jax.numpy as jnp
from jax import lax
from jax.experimental import pallas as pl
from jax.experimental.pallas import tpu as pltpu
from jax.sharding import PartitionSpec as P

CHUNK = 2
WINDOW = 4


def chunk_list(terms):
    chunks = []
    for second in reversed(range(terms)):
        first = 0
        while first <= second:
            number = min(CHUNK, second + 1 - first)
            chunks.append((second, first, number))
            first += number
    return chunks


def one_action(term, here, before, after, across, opposite, kappa):
    value = here.astype(jnp.float32)
    if term == 0:
        stencil = 2.0 * value - before.astype(jnp.float32) - after.astype(jnp.float32)
    elif term == 1:
        stencil = jnp.dot(here, across, preferred_element_type=jnp.float32)
    elif term == 2:
        stencil = value - before.astype(jnp.float32)
    elif term == 3:
        stencil = value - after.astype(jnp.float32)
    elif term == 4:
        stencil = jnp.dot(here, opposite, preferred_element_type=jnp.float32)
    else:
        stencil = value
    return (kappa * stencil).astype(jnp.bfloat16)


def coded(value, floor=1e-30):
    peak = jnp.maximum(jnp.max(jnp.abs(value), axis=0, keepdims=True), floor)
    return jnp.round(value * (32000.0 / peak)), peak * (1.0 / 32000.0)


def short(code):
    return code.astype(jnp.int32).astype(jnp.int16)


def wide(code):
    return code.astype(jnp.int32).astype(jnp.float32)


def gram_kernel(terms, highs, own, slabs_dev, total_cells, *refs):
    basis, region, index, table, out = refs[:5]
    chunks = chunk_list(terms)
    count = len(chunks)
    field, packed, weights, mine, lhs1, lhs2, lhs3, act1, act2, act3, whole2, whole3 = refs[5:17]
    at = 17
    acc = refs[at : at + terms]
    at += terms
    buffers = []
    for _ in range(14):
        buffers.append(refs[at : at + count])
        at += count
    (codes1, got1, scale1, gots1, codes2, got2, scale2, gots2) = buffers[:8]
    (codes3, got3, scale3, gots3, mid, keep) = buffers[8:]
    lvl = refs[at : at + 4]
    lvl_in = refs[at + 4 : at + 8]
    at += 8
    (load_sem, xs, xr, sib_s, sib_r, rel_s, rel_r, hs, hr, hrel_s, hrel_r, ks, kr) = refs[at : at + 13]
    at += 13
    (cs1, cr1, ss1, sr1, cs2, cr2, ss2, sr2, cs3, cr3, ss3, sr3) = refs[at : at + 12]
    lvl_s = refs[at + 12 : at + 16]
    lvl_r = refs[at + 16 : at + 20]

    rows, width = field.shape[1], field.shape[2]
    entries = table.shape[0]
    span = 2 * slabs_dev
    stride = span + 2
    chips = 8 * highs
    local = 4 * highs * own
    half = local // 2
    quarter = local // 4
    me = lax.axis_index("mode")
    chip = me // 2
    core = me % 2
    x = chip % 2
    y = (chip // 2) % 2
    level_z = chip // 4
    low = level_z % 2
    high = level_z // 2

    def across_pair(c):
        return c + 4 - 8 * ((c // 4) % 2)

    def device(c):
        return c * 2 + core

    other = across_pair(chip)
    step = 2 * core - 1
    ahead = lax.rem(chip + chips + step, chips)
    behind = lax.rem(chip + chips - step, chips)
    other_ahead = across_pair(lax.rem(other + chips + step, chips))
    other_behind = across_pair(lax.rem(other + chips - step, chips))
    sibling = chip * 2 + 1 - core
    partner = device(other)
    cross = other * 2 + 1 - core
    x_peer = device(chip + 1 - 2 * x)
    y_peer = device(chip + 2 - 4 * y)

    def high_peer(d):
        return device(chip + 8 * (lax.rem(high + d, highs) - high))

    def remote(src, dst, send, recv, peer):
        return pltpu.make_async_remote_copy(
            src_ref=src,
            dst_ref=dst,
            send_sem=send,
            recv_sem=recv,
            device_id={"mode": peer},
            device_id_type=pl.DeviceIdType.MESH,
        )

    first_slot = 1 + core * slabs_dev
    loads = [
        pltpu.make_async_copy(
            basis.at[:, pl.ds(s * width, width)], field.at[first_slot + s], load_sem.at[s]
        )
        for s in range(slabs_dev)
    ]
    for copy in loads:
        copy.start()

    barrier = pltpu.get_barrier_semaphore()
    greeted = [sibling, partner, cross, x_peer, y_peer]
    greeted += [high_peer(d) for d in range(1, highs)]
    greeted += [device(c) for c in (ahead, behind, other_ahead, other_behind)]
    for peer in greeted:
        pl.semaphore_signal(
            barrier, inc=1, device_id={"mode": peer}, device_id_type=pl.DeviceIdType.MESH
        )

    tall = weights.shape[1]
    piece = width // slabs_dev
    row_at = lax.broadcasted_iota(jnp.int32, (tall, width), 0)
    lane_at = lax.broadcasted_iota(jnp.int32, (tall, width), 1)
    value = jnp.zeros((tall, width), jnp.float32)
    for s in range(slabs_dev):
        where = region[s]
        lanes = (lane_at >= s * piece) & (lane_at < (s + 1) * piece)
        for term in range(terms):
            entry = index[term, where]
            kappa = jnp.where(entry < entries, table[jnp.minimum(entry, entries - 1)], 0.0)
            value = jnp.where(lanes & (row_at == term), kappa, value)
    packed[core] = value

    wi = lax.broadcasted_iota(jnp.int32, (width, width), 0)
    wj = lax.broadcasted_iota(jnp.int32, (width, width), 1)
    beside_one = jnp.where((wi == wj + 1) | (wj == wi + 1), 1.0, 0.0)
    same = jnp.where(wi == wj, 1.0, 0.0)
    flip = jnp.where(wi + wj == width - 1, 1.0, 0.0)
    across = (2.0 * same - beside_one).astype(jnp.bfloat16)
    opposite = (same - flip).astype(jnp.bfloat16)
    ri = lax.broadcasted_iota(jnp.int32, (local, rows), 0)
    rj = lax.broadcasted_iota(jnp.int32, (local, rows), 1)
    source = ri
    for dx in range(2):
        for dy in range(2):
            for dh in range(highs):
                place = (dx * 2 + dy) * highs + dh
                home_z = lax.rem(high + dh, highs) * 2 + low
                home_y = y + dy - 2 * y * dy
                home_x = x + dx - 2 * x * dx
                home = ((home_z * 2 + home_y) * 2 + home_x) * 2 + core
                source = jnp.where(ri >= place * own, ri + (home * own - place * own), source)
    select = jnp.where(rj == source, 1.0, 0.0).astype(jnp.bfloat16)

    pl.semaphore_wait(barrier, len(greeted))
    for copy in loads:
        copy.wait()

    def turn(k):
        return k + core * (slabs_dev - 1 - 2 * k)

    across_copies = []
    relays = []
    for k in range(slabs_dev):
        slot = first_slot + turn(k)
        across_copies.append(
            remote(field.at[slot], field.at[stride + slot], xs.at[k], xr.at[k], partner)
        )
        slot = stride + slot
        relays.append(remote(field.at[slot], field.at[slot], rel_s.at[k], rel_r.at[k], sibling))
    block = pl.ds(first_slot, slabs_dev)
    beside = remote(field.at[block], field.at[block], sib_s.at[0], sib_r.at[0], sibling)
    edge = 1 + core * (span - 1)
    beyond = (1 - core) * (span + 1)
    halos = []
    halo_relays = []
    for n, target in enumerate((ahead, other_ahead)):
        halos.append(
            remote(
                field.at[n * stride + edge],
                field.at[n * stride + beyond],
                hs.at[n],
                hr.at[n],
                device(target),
            )
        )
        slot = n * stride + beyond
        halo_relays.append(
            remote(field.at[slot], field.at[slot], hrel_s.at[n], hrel_r.at[n], sibling)
        )
    small = [
        remote(packed.at[core], packed.at[core + shift], ks.at[n], kr.at[n], peer)
        for n, (peer, shift) in enumerate(((sibling, 0), (partner, 2), (cross, 2)))
    ]
    for copy in small:
        copy.start()
    across_copies[0].start()
    halos[0].start()
    beside.start()
    for copy in across_copies[1:]:
        copy.start()

    def pick(first, number):
        for s in range(number):
            mine[first + s] = jnp.dot(
                select, field[first + s], preferred_element_type=jnp.float32
            ).astype(jnp.bfloat16)

    def acted(term, source_ref, spot):
        part, slab = spot
        alone = term in (1, 4, 5)
        slot = part * stride + 1 + slab
        return one_action(
            term,
            source_ref[slot],
            None if alone else source_ref[slot - 1],
            None if alone else source_ref[slot + 1],
            across,
            opposite,
            weights[part * span + slab, term : term + 1, :],
        )

    lvl[0][...] = jnp.zeros_like(lvl[0])

    def own_actions(lhs, part):
        for term in range(terms):
            squares = None
            for s, spot in enumerate(part):
                value = acted(term, mine, spot)
                lhs[term * local : (term + 1) * local, s * width : (s + 1) * width] = value
                value = value.astype(jnp.float32)
                squares = value * value if squares is None else squares + value * value
            lvl[0][term : term + 1, :] += jnp.sum(squares, axis=0, keepdims=True)

    def all_actions(act, part, second):
        for s, spot in enumerate(part):
            act[second % 2, :, s * width : (s + 1) * width] = acted(second, field, spot)

    def product(lhs, act, second):
        return lax.dot_general(
            lhs[0 : (second + 1) * local, :],
            act[second % 2],
            (((1,), (1,)), ((), ())),
            preferred_element_type=jnp.float32,
        )

    sends = []

    def spread(n, peers):
        copies = [
            remote(lvl[n], lvl_in[n].at[d], lvl_s[n].at[d], lvl_r[n].at[d], peer)
            for d, peer in enumerate(peers)
        ]
        for copy in copies:
            copy.start()
        sends.extend(copies)
        return copies

    def gathered(n, copies):
        for copy in copies:
            copy.wait_recv()
        total = lvl[n][...]
        for d in range(len(copies)):
            total = total + lvl_in[n][d]
        return total

    ends = slabs_dev - 2
    part1 = [(0, s) for s in range(span)]
    part2 = [(1, s) for s in range(span) if s < ends or s >= span - ends]
    part3 = [(1, s) for s in range(ends, span - ends)]
    order = list(reversed(range(terms)))

    halos[0].wait_recv()
    halo_relays[0].start()
    beside.wait()
    for copy in small:
        copy.wait()
    for n in range(4):
        source_value = packed[n]
        for s in range(slabs_dev):
            lanes = (lane_at >= s * piece) & (lane_at < (s + 1) * piece)
            value = jnp.where(lanes, source_value, 0.0)
            shift = piece
            while shift < width:
                value = value + pltpu.roll(value, shift, 1)
                shift *= 2
            weights[n * slabs_dev + s] = value
    across_copies[0].wait_recv()
    relays[0].start()
    halos[1].start()
    halo_relays[0].wait_recv()
    pick(0, stride)
    own_actions(lhs1, part1)
    for n, second in enumerate(order):
        all_actions(act1, part1, second)
        acc[second][...] = product(lhs1, act1, second)
        if n == 0:
            across_copies[1].wait_recv()
            relays[1].start()
        if n == 1:
            halos[1].wait_recv()
            halo_relays[1].start()
        if 2 <= n < slabs_dev - 1 + 0:
            across_copies[n].wait_recv()
            relays[n].start()
    for copy in relays[: slabs_dev - 1] + [halo_relays[1]]:
        copy.wait_recv()
    pick(stride, ends + 2)
    pick(stride + span - ends, ends + 2)
    own_actions(lhs2, part2)
    for n, second in enumerate(order):
        all_actions(act2, part2, second)
        acc[second][...] += product(lhs2, act2, second)
        if n == 2:
            across_copies[slabs_dev - 1].wait_recv()
            relays[slabs_dev - 1].start()
    relays[slabs_dev - 1].wait_recv()
    pick(stride + ends + 2, span - 2 * ends - 2)
    own_actions(lhs3, part3)
    level_copies = spread(0, [x_peer])

    stage1 = []
    stage2 = []
    stage3 = []

    def exchange(n, src, dst, scale, gots, sems, peer):
        cs, cr, ss, sr = sems
        return [
            remote(scale[n], gots[n], ss.at[n], sr.at[n], peer),
            remote(src[n], dst[n], cs.at[n], cr.at[n], peer),
        ]

    for turn_at, second in enumerate(order):
        all_actions(act3, part3, second)
        acc[second][...] += product(lhs3, act3, second)
        if turn_at == 0:
            lvl[1][...] = gathered(0, level_copies)
            level_copies = spread(1, [y_peer])
        if turn_at == 2:
            lvl[2][...] = gathered(1, level_copies)
            level_copies = spread(2, [sibling, partner, cross])
        if turn_at == 4:
            lvl[3][...] = gathered(2, level_copies)
            level_copies = spread(3, [high_peer(d) for d in range(1, highs)])
        for n, (chunk_second, first, number) in enumerate(chunks):
            if chunk_second != second:
                continue
            for i in range(number):
                base = (first + i) * local
                if n % 2 == 0:
                    value = acc[second][base + half : base + local, :]
                else:
                    value = jnp.concatenate(
                        [
                            acc[second][base + quarter : base + half, :],
                            acc[second][base + half + quarter : base + local, :],
                        ],
                        axis=0,
                    )
                code, scale = coded(value)
                codes1[n][i * half : (i + 1) * half, :] = short(code)
                scale1[n][i : i + 1, :] = scale
            stage1.append(
                exchange(
                    n,
                    codes1,
                    got1,
                    scale1,
                    gots1,
                    (cs1, cr1, ss1, sr1),
                    x_peer if n % 2 == 0 else y_peer,
                )
            )
            if n < WINDOW:
                for copy in stage1[n]:
                    copy.start()

    def middle(n):
        second, first, number = chunks[n]
        for copy in stage1[n]:
            copy.wait_recv()
        for i in range(number):
            base = (first + i) * local
            if n % 2 == 0:
                value = acc[second][base : base + half, :]
            else:
                value = jnp.concatenate(
                    [
                        acc[second][base : base + quarter, :],
                        acc[second][base + half : base + half + quarter, :],
                    ],
                    axis=0,
                )
            value = value + wide(got1[n][i * half : (i + 1) * half, :]) * gots1[n][i : i + 1, :]
            mid[n][i * quarter : (i + 1) * quarter, :] = value[0:quarter]
            code, scale = coded(value[quarter:])
            scale2[n][i : i + 1, :] = scale
            whole2[i * quarter : (i + 1) * quarter, :] = code
        codes2[n][...] = short(whole2[0 : number * quarter, :])
        copies = exchange(
            n,
            codes2,
            got2,
            scale2,
            gots2,
            (cs2, cr2, ss2, sr2),
            y_peer if n % 2 == 0 else x_peer,
        )
        for copy in copies:
            copy.start()
        stage2.append(copies)
        if n + WINDOW < count:
            for copy in stage1[n + WINDOW]:
                copy.start()

    def last(n):
        second, first, number = chunks[n]
        for copy in stage2[n]:
            copy.wait_recv()
        opened = wide(got2[n][...])
        for i in range(number):
            part = slice(i * quarter, (i + 1) * quarter)
            value = mid[n][part, :] + opened[part, :] * gots2[n][i : i + 1, :]
            keep[n][i * own : (i + 1) * own, :] = value[0:own]
            code, scale = coded(value[own:])
            scale3[n][i : i + 1, :] = scale
            for d in range(1, highs):
                whole3[d - 1, i * own : (i + 1) * own, :] = code[(d - 1) * own : d * own]
        copies = []
        for d in range(1, highs):
            codes3[n][d - 1] = short(whole3[d - 1, 0 : number * own, :])
            sem = n * (highs - 1) + d - 1
            copies.append(
                remote(scale3[n], gots3[n].at[d - 1], ss3.at[sem], sr3.at[sem], high_peer(d))
            )
            copies.append(
                remote(
                    codes3[n].at[d - 1], got3[n].at[d - 1], cs3.at[sem], cr3.at[sem], high_peer(d)
                )
            )
        for copy in copies:
            copy.start()
        stage3.append(copies)

    def finish(n, level):
        second, first, number = chunks[n]
        for copy in stage3[n]:
            copy.wait_recv()
        opened = [wide(got3[n][d - 1]) for d in range(1, highs)]
        for i in range(number):
            q = first + i
            value = keep[n][i * own : (i + 1) * own, :]
            for d in range(1, highs):
                value = value + (
                    opened[d - 1][i * own : (i + 1) * own, :] * gots3[n][d - 1, i : i + 1, :]
                )
            factor = 1.0 / (total_cells * jnp.sqrt(level[q : q + 1] * level[second : second + 1]))
            pair = q * terms - q * (q - 1) // 2 + second - q
            out[pair] = value * factor

    level = None
    for t in range(count + 5):
        if t < count:
            middle(t)
        if 0 <= t - 2 < count:
            last(t - 2)
        if t == 3:
            total = gathered(3, level_copies)
            level = jnp.sum(total, axis=1, keepdims=True) / (rows * total_cells) + 1e-06
        if 0 <= t - 5 < count:
            finish(t - 5, level)
    for copies in stage1 + stage2 + stage3:
        sends.extend(copies)
    for copy in sends + across_copies + relays + halos + halo_relays:
        copy.wait_send()


def per_device(basis, slab_region, coef_index, coef_table):
    terms = coef_index.shape[1]
    rows, cells_dev = basis.shape
    slabs_dev = slab_region.shape[0]
    width = cells_dev // slabs_dev
    devices = lax.axis_size("mode")
    highs = devices // 16
    own = rows // devices
    span = slabs_dev * 2
    local = 4 * highs * own
    half, quarter = local // 2, local // 4
    sizes = [number for _, _, number in chunk_list(terms)]
    count = len(sizes)
    tall = terms + -terms % 8
    f32, b16, i16 = jnp.float32, jnp.bfloat16, jnp.int16
    ends = slabs_dev - 2
    depths = [span * width, 2 * ends * width, (span - 2 * ends) * width]
    dma = pltpu.SemaphoreType.DMA
    vmem = pltpu.VMEM
    scratch = [
        vmem((2 * (span + 2), rows, width), b16),
        vmem((4, tall, width), f32),
        vmem((2 * span, tall, width), f32),
        vmem((2 * (span + 2), local, width), b16),
    ]
    scratch += [vmem((terms * local, k), b16) for k in depths]
    scratch += [vmem((2, rows, k), b16) for k in depths]
    scratch += [vmem((CHUNK * quarter, rows), f32), vmem((highs - 1, CHUNK * own, rows), f32)]
    scratch += [vmem(((q + 1) * local, rows), f32) for q in range(terms)]
    for size in (half, quarter):
        scratch += [vmem((n * size, rows), i16) for n in sizes] * 2
        scratch += [vmem((n, rows), f32) for n in sizes] * 2
    scratch += [vmem((highs - 1, n * own, rows), i16) for n in sizes] * 2
    scratch += [vmem((n, rows), f32) for n in sizes]
    scratch += [vmem((highs - 1, n, rows), f32) for n in sizes]
    scratch += [vmem((n * quarter, rows), f32) for n in sizes]
    scratch += [vmem((n * own, rows), f32) for n in sizes]
    fans = (1, 1, 3, highs - 1)
    scratch += [vmem((tall, width), f32)] * 4
    scratch += [vmem((n, tall, width), f32) for n in fans]
    scratch += [dma((slabs_dev,))] * 3
    scratch += [dma((1,))] * 2
    scratch += [dma((slabs_dev,))] * 2
    scratch += [dma((2,))] * 4
    scratch += [dma((3,))] * 2
    scratch += [dma((count,))] * 8
    scratch += [dma((count * (highs - 1),))] * 4
    scratch += [dma((n,)) for n in fans] * 2
    smem = pl.BlockSpec(memory_space=pltpu.SMEM)
    return pl.pallas_call(
        functools.partial(gram_kernel, terms, highs, own, slabs_dev, cells_dev * devices),
        out_shape=jax.ShapeDtypeStruct((terms * (terms + 1) // 2, own, rows), f32),
        in_specs=[pl.BlockSpec(memory_space=pl.ANY), smem, smem, smem],
        out_specs=pl.BlockSpec(memory_space=pltpu.VMEM),
        scratch_shapes=scratch,
        compiler_params=pltpu.CompilerParams(
            collective_id=0, has_side_effects=True, vmem_limit_bytes=62 << 20
        ),
    )(basis, slab_region, coef_index.T, coef_table)


def solution(mesh):
    return jax.shard_map(
        per_device,
        mesh=mesh,
        in_specs=(P("groups", "mode"), P(("groups", "mode")), P("groups", None), P("groups")),
        out_specs=P(None, ("groups", "mode"), None),
        check_vma=False,
    )
```

```python
import functools

import jax
import jax.numpy as jnp
from jax import lax
from jax.experimental import pallas as pl
from jax.experimental.pallas import tpu as pltpu
from jax.sharding import PartitionSpec as P

CHUNK = 2
WINDOW = 4


def chunk_list(terms):
    chunks = []
    for second in reversed(range(terms)):
        first = 0
        while first <= second:
            number = min(CHUNK, second + 1 - first)
            chunks.append((second, first, number))
            first += number
    return chunks


def one_action(term, here, before, after, across, opposite, kappa):
    value = here.astype(jnp.float32)
    if term == 0:
        stencil = 2.0 * value - before.astype(jnp.float32) - after.astype(jnp.float32)
    elif term == 1:
        stencil = jnp.dot(here, across, preferred_element_type=jnp.float32)
    elif term == 2:
        stencil = value - before.astype(jnp.float32)
    elif term == 3:
        stencil = value - after.astype(jnp.float32)
    elif term == 4:
        stencil = jnp.dot(here, opposite, preferred_element_type=jnp.float32)
    else:
        stencil = value
    return (kappa * stencil).astype(jnp.bfloat16)


def coded(value, floor=1e-30):
    peak = jnp.maximum(jnp.max(jnp.abs(value), axis=0, keepdims=True), floor)
    return jnp.round(value * (32000.0 / peak)), peak * (1.0 / 32000.0)


def short(code):
    return code.astype(jnp.int32).astype(jnp.int16)


def wide(code):
    return code.astype(jnp.int32).astype(jnp.float32)


def gram_kernel(terms, highs, own, slabs_dev, total_cells, *refs):
    basis, region_in, index_in, table_in, out = refs[:5]
    chunks = chunk_list(terms)
    count = len(chunks)
    field, packed, weights, mine, lhs1, lhs2, lhs3, act1, act2, act3, whole2, whole3 = refs[5:17]
    at = 17
    acc = refs[at : at + terms]
    at += terms
    buffers = []
    for _ in range(14):
        buffers.append(refs[at : at + count])
        at += count
    (codes1, got1, scale1, gots1, codes2, got2, scale2, gots2) = buffers[:8]
    (codes3, got3, scale3, gots3, mid, keep) = buffers[8:]
    lvl = refs[at : at + 5]
    lvl_in = refs[at + 5 : at + 10]
    region, index, table, heard = refs[at + 10 : at + 14]
    at += 14
    (load_sem, xs, xr, sib_s, sib_r, rel_s, rel_r, hs, hr, hrel_s, hrel_r, ks, kr) = refs[at : at + 13]
    at += 13
    (cs1, cr1, ss1, sr1, cs2, cr2, ss2, sr2, cs3, cr3, ss3, sr3) = refs[at : at + 12]
    lvl_s = refs[at + 12 : at + 17]
    lvl_r = refs[at + 17 : at + 22]

    rows, width = field.shape[1], field.shape[2]
    entries = table_in.shape[0]
    span = 2 * slabs_dev
    stride = span + 2
    chips = 8 * highs
    local = 4 * highs * own
    half = local // 2
    quarter = local // 4
    me = lax.axis_index("mode")
    chip = me // 2
    core = me % 2
    x = chip % 2
    y = (chip // 2) % 2
    level_z = chip // 4
    low = level_z % 2
    high = level_z // 2

    def across_pair(c):
        return c + 4 - 8 * ((c // 4) % 2)

    def device(c):
        return c * 2 + core

    other = across_pair(chip)
    step = 2 * core - 1
    ahead = lax.rem(chip + chips + step, chips)
    behind = lax.rem(chip + chips - step, chips)
    other_ahead = across_pair(lax.rem(other + chips + step, chips))
    other_behind = across_pair(lax.rem(other + chips - step, chips))
    sibling = chip * 2 + 1 - core
    partner = device(other)
    x_peer = device(chip + 1 - 2 * x)
    y_peer = device(chip + 2 - 4 * y)

    def high_peer(d):
        return device(chip + 8 * (lax.rem(high + d, highs) - high))

    def remote(src, dst, send, recv, peer):
        return pltpu.make_async_remote_copy(
            src_ref=src,
            dst_ref=dst,
            send_sem=send,
            recv_sem=recv,
            device_id={"mode": peer},
            device_id_type=pl.DeviceIdType.MESH,
        )

    first_slot = 1 + core * slabs_dev
    loads = [
        pltpu.make_async_copy(
            basis.at[:, pl.ds(s * width, width)], field.at[first_slot + s], load_sem.at[s]
        )
        for s in range(slabs_dev)
    ]
    scalars = [
        pltpu.make_async_copy(src, dst, load_sem.at[slabs_dev + n])
        for n, (src, dst) in enumerate(((region_in, region), (index_in, index), (table_in, table)))
    ]
    for copy in scalars + loads:
        copy.start()

    barrier = pltpu.get_barrier_semaphore()
    linked = [partner, x_peer, y_peer] + [high_peer(d) for d in range(1, highs)]

    def signal(semaphore, peer):
        pl.semaphore_signal(
            semaphore, inc=1, device_id={"mode": peer}, device_id_type=pl.DeviceIdType.MESH
        )

    for peer in linked + [sibling]:
        signal(barrier, peer)
    for copy in scalars:
        copy.wait()

    tall = weights.shape[1]
    piece = width // slabs_dev
    row_at = lax.broadcasted_iota(jnp.int32, (tall, width), 0)
    lane_at = lax.broadcasted_iota(jnp.int32, (tall, width), 1)
    value = jnp.zeros((tall, width), jnp.float32)
    for s in range(slabs_dev):
        where = region[s]
        lanes = (lane_at >= s * piece) & (lane_at < (s + 1) * piece)
        for term in range(terms):
            entry = index[term, where]
            kappa = jnp.where(entry < entries, table[jnp.minimum(entry, entries - 1)], 0.0)
            value = jnp.where(lanes & (row_at == term), kappa, value)
    packed[core] = value

    wi = lax.broadcasted_iota(jnp.int32, (width, width), 0)
    wj = lax.broadcasted_iota(jnp.int32, (width, width), 1)
    beside_one = jnp.where((wi == wj + 1) | (wj == wi + 1), 1.0, 0.0)
    same = jnp.where(wi == wj, 1.0, 0.0)
    flip = jnp.where(wi + wj == width - 1, 1.0, 0.0)
    across = (2.0 * same - beside_one).astype(jnp.bfloat16)
    opposite = (same - flip).astype(jnp.bfloat16)
    ri = lax.broadcasted_iota(jnp.int32, (local, rows), 0)
    rj = lax.broadcasted_iota(jnp.int32, (local, rows), 1)
    source = ri
    for dx in range(2):
        for dy in range(2):
            for dh in range(highs):
                place = (dx * 2 + dy) * highs + dh
                home_z = lax.rem(high + dh, highs) * 2 + low
                home_y = y + dy - 2 * y * dy
                home_x = x + dx - 2 * x * dx
                home = ((home_z * 2 + home_y) * 2 + home_x) * 2 + core
                source = jnp.where(ri >= place * own, ri + (home * own - place * own), source)
    select = jnp.where(rj == source, 1.0, 0.0).astype(jnp.bfloat16)

    pl.semaphore_wait(barrier, len(linked) + 1)
    for copy in loads:
        copy.wait()

    def turn(k):
        return k + core * (slabs_dev - 1 - 2 * k)

    across_copies = []
    relays = []
    for k in range(slabs_dev):
        slot = first_slot + turn(k)
        across_copies.append(
            remote(field.at[slot], field.at[stride + slot], xs.at[k], xr.at[k], partner)
        )
        slot = stride + slot
        relays.append(remote(field.at[slot], field.at[slot], rel_s.at[k], rel_r.at[k], sibling))
    block = pl.ds(first_slot, slabs_dev)
    beside = remote(field.at[block], field.at[block], sib_s.at[0], sib_r.at[0], sibling)
    edge = 1 + core * (span - 1)
    beyond = (1 - core) * (span + 1)
    halos = []
    halo_relays = []
    for n, target in enumerate((ahead, other_ahead)):
        halos.append(
            remote(
                field.at[n * stride + edge],
                field.at[n * stride + beyond],
                hs.at[n],
                hr.at[n],
                device(target),
            )
        )
        slot = n * stride + beyond
        halo_relays.append(
            remote(field.at[slot], field.at[slot], hrel_s.at[n], hrel_r.at[n], sibling)
        )
    small = [
        remote(packed.at[core], packed.at[core + shift], ks.at[n], kr.at[n], peer)
        for n, (peer, shift) in enumerate(((sibling, 0), (partner, 2)))
    ]
    small.append(remote(packed.at[2 + core], packed.at[2 + core], ks.at[2], kr.at[2], sibling))
    for copy in small[:2] + across_copies[:1] + [beside] + across_copies[1:]:
        copy.start()

    def tell(n):
        for peer in linked:
            signal(heard.at[n], peer)

    def hear(n):
        pl.semaphore_wait(heard.at[n], len(linked))

    tell(0)

    def pick(first, number):
        for s in range(number):
            mine[first + s] = jnp.dot(
                select, field[first + s], preferred_element_type=jnp.float32
            ).astype(jnp.bfloat16)

    def acted(term, source_ref, spot):
        part, slab = spot
        alone = term in (1, 4, 5)
        slot = part * stride + 1 + slab
        return one_action(
            term,
            source_ref[slot],
            None if alone else source_ref[slot - 1],
            None if alone else source_ref[slot + 1],
            across,
            opposite,
            weights[part * span + slab, term : term + 1, :],
        )

    lvl[0][...] = jnp.zeros_like(lvl[0])

    def own_actions(lhs, part):
        for term in range(terms):
            squares = None
            for s, spot in enumerate(part):
                value = acted(term, mine, spot)
                lhs[term * local : (term + 1) * local, s * width : (s + 1) * width] = value
                value = value.astype(jnp.float32)
                squares = value * value if squares is None else squares + value * value
            lvl[0][term : term + 1, :] += jnp.sum(squares, axis=0, keepdims=True)

    def all_actions(act, part, second):
        for s, spot in enumerate(part):
            act[second % 2, :, s * width : (s + 1) * width] = acted(second, field, spot)

    def product(lhs, act, second):
        return lax.dot_general(
            lhs[0 : (second + 1) * local, :],
            act[second % 2],
            (((1,), (1,)), ((), ())),
            preferred_element_type=jnp.float32,
        )

    sends = []

    def spread(n, peers):
        copies = [
            remote(lvl[n], lvl_in[n].at[d], lvl_s[n].at[d], lvl_r[n].at[d], peer)
            for d, peer in enumerate(peers)
        ]
        for copy in copies:
            copy.start()
        sends.extend(copies)
        return copies

    def gathered(n, copies):
        for copy in copies:
            copy.wait_recv()
        total = lvl[n][...]
        for d in range(len(copies)):
            total = total + lvl_in[n][d]
        return total

    ends = slabs_dev - 2
    part1 = [(0, s) for s in range(1, span - 1)]
    part2 = [(0, 0), (0, span - 1)]
    part2 += [(1, s) for s in range(span) if s < ends or s >= span - ends]
    part3 = [(1, s) for s in range(ends, span - ends)]
    order = list(reversed(range(terms)))

    def expand(first):
        for n in range(first, first + 2):
            source_value = packed[n]
            for s in range(slabs_dev):
                lanes = (lane_at >= s * piece) & (lane_at < (s + 1) * piece)
                value = jnp.where(lanes, source_value, 0.0)
                shift = piece
                while shift < width:
                    value = value + pltpu.roll(value, shift, 1)
                    shift *= 2
                weights[n * slabs_dev + s] = value

    def pass_on(k):
        across_copies[k].wait_recv()
        relays[k].start()

    small[0].wait()
    expand(0)
    hear(0)
    tell(1)
    beside.wait()
    pick(1, span)
    hear(1)
    tell(2)
    small[1].wait()
    small[2].start()
    own_actions(lhs1, part1)
    hear(2)
    halos[0].start()
    pass_on(0)
    halos[1].start()
    for n, second in enumerate(order):
        all_actions(act1, part1, second)
        acc[second][...] = product(lhs1, act1, second)
        if n < slabs_dev - 2:
            pass_on(n + 1)
        if n in (2, 3):
            halos[n - 2].wait_recv()
            halo_relays[n - 2].start()
    small[2].wait()
    expand(2)
    for copy in relays[: slabs_dev - 1] + halo_relays:
        copy.wait_recv()
    pick(0, 1)
    pick(span + 1, 1)
    pick(stride, ends + 2)
    pick(stride + span - ends, ends + 2)
    own_actions(lhs2, part2)
    for n, second in enumerate(order):
        all_actions(act2, part2, second)
        acc[second][...] += product(lhs2, act2, second)
        if n == 2:
            pass_on(slabs_dev - 1)
    relays[slabs_dev - 1].wait_recv()
    pick(stride + ends + 2, span - 2 * ends - 2)
    own_actions(lhs3, part3)
    level_copies = spread(0, [x_peer])

    stage1 = []
    stage2 = []
    stage3 = []

    def exchange(n, src, dst, scale, gots, sems, peer):
        cs, cr, ss, sr = sems
        return [
            remote(scale[n], gots[n], ss.at[n], sr.at[n], peer),
            remote(src[n], dst[n], cs.at[n], cr.at[n], peer),
        ]

    for second in order:
        all_actions(act3, part3, second)
        acc[second][...] += product(lhs3, act3, second)
        for n, (chunk_second, first, number) in enumerate(chunks):
            if chunk_second != second:
                continue
            for i in range(number):
                base = (first + i) * local
                if n % 2 == 0:
                    value = acc[second][base + half : base + local, :]
                else:
                    value = jnp.concatenate(
                        [
                            acc[second][base + quarter : base + half, :],
                            acc[second][base + half + quarter : base + local, :],
                        ],
                        axis=0,
                    )
                code, scale = coded(value)
                codes1[n][i * half : (i + 1) * half, :] = short(code)
                scale1[n][i : i + 1, :] = scale
            stage1.append(
                exchange(
                    n,
                    codes1,
                    got1,
                    scale1,
                    gots1,
                    (cs1, cr1, ss1, sr1),
                    x_peer if n % 2 == 0 else y_peer,
                )
            )
            if n < WINDOW:
                for copy in stage1[n]:
                    copy.start()

    def middle(n):
        second, first, number = chunks[n]
        for copy in stage1[n]:
            copy.wait_recv()
        for i in range(number):
            base = (first + i) * local
            if n % 2 == 0:
                value = acc[second][base : base + half, :]
            else:
                value = jnp.concatenate(
                    [
                        acc[second][base : base + quarter, :],
                        acc[second][base + half : base + half + quarter, :],
                    ],
                    axis=0,
                )
            value = value + wide(got1[n][i * half : (i + 1) * half, :]) * gots1[n][i : i + 1, :]
            mid[n][i * quarter : (i + 1) * quarter, :] = value[0:quarter]
            code, scale = coded(value[quarter:])
            scale2[n][i : i + 1, :] = scale
            whole2[i * quarter : (i + 1) * quarter, :] = code
        codes2[n][...] = short(whole2[0 : number * quarter, :])
        copies = exchange(
            n,
            codes2,
            got2,
            scale2,
            gots2,
            (cs2, cr2, ss2, sr2),
            y_peer if n % 2 == 0 else x_peer,
        )
        for copy in copies:
            copy.start()
        stage2.append(copies)
        if n + WINDOW < count:
            for copy in stage1[n + WINDOW]:
                copy.start()

    def last(n):
        second, first, number = chunks[n]
        for copy in stage2[n]:
            copy.wait_recv()
        opened = wide(got2[n][...])
        for i in range(number):
            part = slice(i * quarter, (i + 1) * quarter)
            value = mid[n][part, :] + opened[part, :] * gots2[n][i : i + 1, :]
            keep[n][i * own : (i + 1) * own, :] = value[0:own]
            code, scale = coded(value[own:])
            scale3[n][i : i + 1, :] = scale
            for d in range(1, highs):
                whole3[d - 1, i * own : (i + 1) * own, :] = code[(d - 1) * own : d * own]
        copies = []
        for d in range(1, highs):
            codes3[n][d - 1] = short(whole3[d - 1, 0 : number * own, :])
            sem = n * (highs - 1) + d - 1
            copies.append(
                remote(scale3[n], gots3[n].at[d - 1], ss3.at[sem], sr3.at[sem], high_peer(d))
            )
            copies.append(
                remote(
                    codes3[n].at[d - 1], got3[n].at[d - 1], cs3.at[sem], cr3.at[sem], high_peer(d)
                )
            )
        for copy in copies:
            copy.start()
        stage3.append(copies)

    def finish(n, level):
        second, first, number = chunks[n]
        for copy in stage3[n]:
            copy.wait_recv()
        opened = [wide(got3[n][d - 1]) for d in range(1, highs)]
        for i in range(number):
            q = first + i
            value = keep[n][i * own : (i + 1) * own, :]
            for d in range(1, highs):
                value = value + (
                    opened[d - 1][i * own : (i + 1) * own, :] * gots3[n][d - 1, i : i + 1, :]
                )
            factor = 1.0 / (total_cells * jnp.sqrt(level[q : q + 1] * level[second : second + 1]))
            pair = q * terms - q * (q - 1) // 2 + second - q
            out[pair] = value * factor

    level = None
    finished = 0
    for t in range(count + 8):
        if t < count:
            middle(t)
        if t == 0:
            lvl[1][...] = gathered(0, level_copies)
            level_copies = spread(1, [y_peer])
        if 0 <= t - 4 < count:
            last(t - 4)
        if t == 4:
            lvl[2][...] = gathered(1, level_copies)
            level_copies = spread(2, [high_peer(d) for d in range(1, highs)])
        if t == 7:
            lvl[3][...] = gathered(2, level_copies)
            level_copies = spread(3, [partner])
        if t == 8:
            lvl[4][...] = gathered(3, level_copies)
            level_copies = spread(4, [sibling])
        if t == 10:
            total = gathered(4, level_copies)
            level = jnp.sum(total, axis=1, keepdims=True) / (rows * total_cells) + 1e-06
        while t >= 10 and finished <= t - 8 and finished < count:
            finish(finished, level)
            finished += 1
    for copies in stage1 + stage2 + stage3:
        sends.extend(copies)
    for copy in sends + across_copies + relays + halos + halo_relays:
        copy.wait_send()


def per_device(basis, slab_region, coef_index, coef_table):
    terms = coef_index.shape[1]
    rows, cells_dev = basis.shape
    slabs_dev = slab_region.shape[0]
    width = cells_dev // slabs_dev
    devices = lax.axis_size("mode")
    highs = devices // 16
    own = rows // devices
    span = slabs_dev * 2
    local = 4 * highs * own
    half, quarter = local // 2, local // 4
    sizes = [number for _, _, number in chunk_list(terms)]
    count = len(sizes)
    tall = terms + -terms % 8
    f32, b16, i16 = jnp.float32, jnp.bfloat16, jnp.int16
    ends = slabs_dev - 2
    depths = [(span - 2) * width, (2 * ends + 2) * width, (span - 2 * ends) * width]
    dma = pltpu.SemaphoreType.DMA
    vmem = pltpu.VMEM
    scratch = [
        vmem((2 * (span + 2), rows, width), b16),
        vmem((4, tall, width), f32),
        vmem((2 * span, tall, width), f32),
        vmem((2 * (span + 2), local, width), b16),
    ]
    scratch += [vmem((terms * local, k), b16) for k in depths]
    scratch += [vmem((2, rows, k), b16) for k in depths]
    scratch += [vmem((CHUNK * quarter, rows), f32), vmem((highs - 1, CHUNK * own, rows), f32)]
    scratch += [vmem(((q + 1) * local, rows), f32) for q in range(terms)]
    for size in (half, quarter):
        scratch += [vmem((n * size, rows), i16) for n in sizes] * 2
        scratch += [vmem((n, rows), f32) for n in sizes] * 2
    scratch += [vmem((highs - 1, n * own, rows), i16) for n in sizes] * 2
    scratch += [vmem((n, rows), f32) for n in sizes]
    scratch += [vmem((highs - 1, n, rows), f32) for n in sizes]
    scratch += [vmem((n * quarter, rows), f32) for n in sizes]
    scratch += [vmem((n * own, rows), f32) for n in sizes]
    fans = (1, 1, highs - 1, 1, 1)
    scratch += [vmem((tall, width), f32)] * 5
    scratch += [vmem((n, tall, width), f32) for n in fans]
    scratch += [
        pltpu.SMEM(slab_region.shape, jnp.int32),
        pltpu.SMEM(coef_index.shape[::-1], jnp.int32),
        pltpu.SMEM(coef_table.shape, f32),
        pltpu.SemaphoreType.REGULAR((3,)),
        dma((slabs_dev + 3,)),
    ]
    scratch += [dma((slabs_dev,))] * 2
    scratch += [dma((1,))] * 2
    scratch += [dma((slabs_dev,))] * 2
    scratch += [dma((2,))] * 4
    scratch += [dma((3,))] * 2
    scratch += [dma((count,))] * 8
    scratch += [dma((count * (highs - 1),))] * 4
    scratch += [dma((n,)) for n in fans] * 2
    return pl.pallas_call(
        functools.partial(gram_kernel, terms, highs, own, slabs_dev, cells_dev * devices),
        out_shape=jax.ShapeDtypeStruct((terms * (terms + 1) // 2, own, rows), f32),
        in_specs=[pl.BlockSpec(memory_space=pltpu.HBM)] * 4,
        out_specs=pl.BlockSpec(memory_space=pltpu.VMEM),
        scratch_shapes=scratch,
        compiler_params=pltpu.CompilerParams(
            collective_id=0, has_side_effects=True, vmem_limit_bytes=62 << 20
        ),
    )(basis, slab_region, coef_index.T, coef_table)


def solution(mesh):
    return jax.shard_map(
        per_device,
        mesh=mesh,
        in_specs=(P("groups", "mode"), P(("groups", "mode")), P("groups", None), P("groups")),
        out_specs=P(None, ("groups", "mode"), None),
        check_vma=False,
    )
```

```python
import functools

import jax
import jax.numpy as jnp
from jax import lax
from jax.experimental import pallas as pl
from jax.experimental.pallas import tpu as pltpu
from jax.sharding import PartitionSpec as P

CHUNK = 2
WINDOW = 4
EARLY = 0
LAG = 4


def chunk_list(terms):
    chunks = []
    for second in range(terms):
        first = 0
        while first <= second:
            number = min(CHUNK, second + 1 - first)
            chunks.append((second, first, number))
            first += number
    return chunks


def one_action(term, here, before, after, across, opposite, kappa):
    value = here.astype(jnp.float32)
    if term == 0:
        stencil = 2.0 * value - before.astype(jnp.float32) - after.astype(jnp.float32)
    elif term == 1:
        stencil = jnp.dot(here, across, preferred_element_type=jnp.float32)
    elif term == 2:
        stencil = value - before.astype(jnp.float32)
    elif term == 3:
        stencil = value - after.astype(jnp.float32)
    elif term == 4:
        stencil = jnp.dot(here, opposite, preferred_element_type=jnp.float32)
    else:
        stencil = value
    return (kappa * stencil).astype(jnp.bfloat16)


def coded(value, floor=1e-30):
    peak = jnp.maximum(jnp.max(jnp.abs(value), axis=0, keepdims=True), floor)
    return jnp.round(value * (32000.0 / peak)), peak * (1.0 / 32000.0)


def short(code):
    return code.astype(jnp.int32).astype(jnp.int16)


def wide(code):
    return code.astype(jnp.int32).astype(jnp.float32)


def gram_kernel(terms, highs, own, slabs_dev, total_cells, *refs):
    basis, region_in, index_in, table_in, out = refs[:5]
    chunks = chunk_list(terms)
    count = len(chunks)
    field, packed, weights, mine, lhs1, lhs2, lhs3, act1, act2, act3, whole2, whole3 = refs[5:17]
    at = 17
    acc = refs[at : at + terms]
    at += terms
    buffers = []
    for _ in range(14):
        buffers.append(refs[at : at + count])
        at += count
    (codes1, got1, scale1, gots1, codes2, got2, scale2, gots2) = buffers[:8]
    (codes3, got3, scale3, gots3, mid, keep) = buffers[8:]
    lvl = refs[at : at + 5]
    lvl_in = refs[at + 5 : at + 10]
    region, index, table, heard = refs[at + 10 : at + 14]
    at += 14
    (load_sem, xs, xr, sib_s, sib_r, rel_s, rel_r, hs, hr, hrel_s, hrel_r, ks, kr) = refs[at : at + 13]
    at += 13
    (cs1, cr1, ss1, sr1, cs2, cr2, ss2, sr2, cs3, cr3, ss3, sr3) = refs[at : at + 12]
    lvl_s = refs[at + 12 : at + 17]
    lvl_r = refs[at + 17 : at + 22]

    rows, width = field.shape[1], field.shape[2]
    entries = table_in.shape[0]
    span = 2 * slabs_dev
    stride = span + 2
    chips = 8 * highs
    local = 4 * highs * own
    half = local // 2
    quarter = local // 4
    me = lax.axis_index("mode")
    chip = me // 2
    core = me % 2
    x = chip % 2
    y = (chip // 2) % 2
    level_z = chip // 4
    low = level_z % 2
    high = level_z // 2

    def across_pair(c):
        return c + 4 - 8 * ((c // 4) % 2)

    def device(c):
        return c * 2 + core

    other = across_pair(chip)
    step = 2 * core - 1
    ahead = lax.rem(chip + chips + step, chips)
    other_next = lax.rem(other + chips + step, chips)
    sibling = chip * 2 + 1 - core
    partner = device(other)
    x_peer = device(chip + 1 - 2 * x)
    y_peer = device(chip + 2 - 4 * y)

    def high_peer(d):
        return device(chip + 8 * (lax.rem(high + d, highs) - high))

    def remote(src, dst, send, recv, peer):
        return pltpu.make_async_remote_copy(
            src_ref=src,
            dst_ref=dst,
            send_sem=send,
            recv_sem=recv,
            device_id={"mode": peer},
            device_id_type=pl.DeviceIdType.MESH,
        )

    first_slot = 1 + core * slabs_dev
    loads = [
        pltpu.make_async_copy(
            basis.at[:, pl.ds(s * width, width)], field.at[first_slot + s], load_sem.at[s]
        )
        for s in range(slabs_dev)
    ]
    scalars = [
        pltpu.make_async_copy(src, dst, load_sem.at[slabs_dev + n])
        for n, (src, dst) in enumerate(((region_in, region), (index_in, index), (table_in, table)))
    ]
    for copy in scalars + loads:
        copy.start()

    barrier = pltpu.get_barrier_semaphore()
    linked = [partner, x_peer, y_peer] + [high_peer(d) for d in range(1, highs)]

    def signal(semaphore, peer):
        pl.semaphore_signal(
            semaphore, inc=1, device_id={"mode": peer}, device_id_type=pl.DeviceIdType.MESH
        )

    for peer in linked + [sibling]:
        signal(barrier, peer)
    for copy in scalars:
        copy.wait()

    tall = weights.shape[1]
    piece = width // slabs_dev
    row_at = lax.broadcasted_iota(jnp.int32, (tall, width), 0)
    lane_at = lax.broadcasted_iota(jnp.int32, (tall, width), 1)
    value = jnp.zeros((tall, width), jnp.float32)
    for s in range(slabs_dev):
        where = region[s]
        lanes = (lane_at >= s * piece) & (lane_at < (s + 1) * piece)
        for term in range(terms):
            entry = index[term, where]
            kappa = jnp.where(entry < entries, table[jnp.minimum(entry, entries - 1)], 0.0)
            value = jnp.where(lanes & (row_at == term), kappa, value)
    packed[core] = value

    wi = lax.broadcasted_iota(jnp.int32, (width, width), 0)
    wj = lax.broadcasted_iota(jnp.int32, (width, width), 1)
    beside_one = jnp.where((wi == wj + 1) | (wj == wi + 1), 1.0, 0.0)
    same = jnp.where(wi == wj, 1.0, 0.0)
    flip = jnp.where(wi + wj == width - 1, 1.0, 0.0)
    across = (2.0 * same - beside_one).astype(jnp.bfloat16)
    opposite = (same - flip).astype(jnp.bfloat16)
    ri = lax.broadcasted_iota(jnp.int32, (local, rows), 0)
    rj = lax.broadcasted_iota(jnp.int32, (local, rows), 1)
    source = ri
    for dx in range(2):
        for dy in range(2):
            for dh in range(highs):
                place = (dx * 2 + dy) * highs + dh
                home_z = lax.rem(high + dh, highs) * 2 + low
                home_y = y + dy - 2 * y * dy
                home_x = x + dx - 2 * x * dx
                home = ((home_z * 2 + home_y) * 2 + home_x) * 2 + core
                source = jnp.where(ri >= place * own, ri + (home * own - place * own), source)
    select = jnp.where(rj == source, 1.0, 0.0).astype(jnp.bfloat16)

    pl.semaphore_wait(barrier, len(linked) + 1)
    for copy in loads:
        copy.wait()

    def turn(k):
        return k + core * (slabs_dev - 1 - 2 * k)

    across_copies = []
    relays = []
    for k in range(slabs_dev):
        slot = first_slot + turn(k)
        across_copies.append(
            remote(field.at[slot], field.at[stride + slot], xs.at[k], xr.at[k], partner)
        )
        slot = stride + slot
        relays.append(remote(field.at[slot], field.at[slot], rel_s.at[k], rel_r.at[k], sibling))
    block = pl.ds(first_slot, slabs_dev)
    beside = remote(field.at[block], field.at[block], sib_s.at[0], sib_r.at[0], sibling)
    edge = 1 + core * (span - 1)
    beyond = (1 - core) * (span + 1)
    halos = []
    halo_relays = []
    arrivals = []
    for n, (origin, toward) in enumerate(((chip, ahead), (other, other_next))):
        inside = jnp.where((toward // 4) == (origin // 4) + 1 - 2 * ((origin // 4) % 2), 1, 0)
        landing = n + inside - 2 * n * inside
        target = toward + landing * (across_pair(toward) - toward)
        halos.append(
            remote(
                field.at[n * stride + edge],
                field.at[landing * stride + beyond],
                hs.at[n],
                hr.at[landing],
                device(target),
            )
        )
        slot = n * stride + beyond
        arrivals.append(remote(field.at[slot], field.at[slot], hs.at[n], hr.at[n], partner))
        halo_relays.append(
            remote(field.at[slot], field.at[slot], hrel_s.at[n], hrel_r.at[n], sibling)
        )
    small = [
        remote(packed.at[core], packed.at[core + shift], ks.at[n], kr.at[n], peer)
        for n, (peer, shift) in enumerate(((sibling, 0), (partner, 2)))
    ]
    small.append(remote(packed.at[2 + core], packed.at[2 + core], ks.at[2], kr.at[2], sibling))
    for copy in small[:2] + across_copies[:1] + [beside] + across_copies[1:]:
        copy.start()

    def tell(n):
        for peer in linked:
            signal(heard.at[n], peer)

    def hear(n):
        pl.semaphore_wait(heard.at[n], len(linked))

    tell(0)

    def pick(first, number):
        for s in range(number):
            mine[first + s] = jnp.dot(
                select, field[first + s], preferred_element_type=jnp.float32
            ).astype(jnp.bfloat16)

    def acted(term, source_ref, spot):
        part, slab = spot
        alone = term in (1, 4, 5)
        slot = part * stride + 1 + slab
        return one_action(
            term,
            source_ref[slot],
            None if alone else source_ref[slot - 1],
            None if alone else source_ref[slot + 1],
            across,
            opposite,
            weights[part * span + slab, term : term + 1, :],
        )

    lvl[0][...] = jnp.zeros_like(lvl[0])

    def own_action(lhs, part, term):
        squares = None
        for s, spot in enumerate(part):
            value = acted(term, mine, spot)
            lhs[term * local : (term + 1) * local, s * width : (s + 1) * width] = value
            value = value.astype(jnp.float32)
            squares = value * value if squares is None else squares + value * value
        lvl[0][term : term + 1, :] += jnp.sum(squares, axis=0, keepdims=True)

    def all_actions(act, part, second):
        for s, spot in enumerate(part):
            act[second % 2, :, s * width : (s + 1) * width] = acted(second, field, spot)

    def product(lhs, act, second):
        return lax.dot_general(
            lhs[0 : (second + 1) * local, :],
            act[second % 2],
            (((1,), (1,)), ((), ())),
            preferred_element_type=jnp.float32,
        )

    sends = []

    def spread(n, peers):
        copies = [
            remote(lvl[n], lvl_in[n].at[d], lvl_s[n].at[d], lvl_r[n].at[d], peer)
            for d, peer in enumerate(peers)
        ]
        for copy in copies:
            copy.start()
        sends.extend(copies)
        return copies

    def gathered(n, copies):
        for copy in copies:
            copy.wait_recv()
        total = lvl[n][...]
        for d in range(len(copies)):
            total = total + lvl_in[n][d]
        return total

    ends = slabs_dev - 2
    part1 = [(0, s) for s in range(1, span - 1)]
    part2 = [(1, s) for s in range(1, span - 1) if s < ends or s >= span - ends]
    part3 = [(1, s) for s in range(ends, span - ends)]
    part3 += [(n, s) for n in range(2) for s in (0, span - 1)]
    order = list(range(terms))

    def expand(first):
        for n in range(first, first + 2):
            source_value = packed[n]
            for s in range(slabs_dev):
                lanes = (lane_at >= s * piece) & (lane_at < (s + 1) * piece)
                value = jnp.where(lanes, source_value, 0.0)
                shift = piece
                while shift < width:
                    value = value + pltpu.roll(value, shift, 1)
                    shift *= 2
                weights[n * slabs_dev + s] = value

    def pass_on(k):
        across_copies[k].wait_recv()
        relays[k].start()

    small[0].wait()
    expand(0)
    hear(0)
    tell(1)
    beside.wait()
    pick(1, span)
    hear(1)
    tell(2)
    small[1].wait()
    small[2].start()
    hear(2)
    halos[0].start()
    pass_on(0)
    halos[1].start()
    for second in order:
        own_action(lhs1, part1, second)
        all_actions(act1, part1, second)
        acc[second][...] = product(lhs1, act1, second)
        if second == 2:
            pass_on(1)
    small[2].wait()
    expand(2)
    pass_on(2)
    for copy in relays[: slabs_dev - 1]:
        copy.wait_recv()
    pick(stride + 1, ends + 1)
    pick(stride + span - ends, ends + 1)
    for second in order:
        own_action(lhs2, part2, second)
        all_actions(act2, part2, second)
        acc[second][...] += product(lhs2, act2, second)
        if second == 0:
            for n in range(2):
                arrivals[n].wait_recv()
                halo_relays[n].start()
        if second == 2:
            pass_on(slabs_dev - 1)
    for copy in halo_relays:
        copy.wait_recv()
    for n in range(2):
        pick(n * stride, 1)
        pick(n * stride + span + 1, 1)
    relays[slabs_dev - 1].wait_recv()
    pick(stride + ends + 2, span - 2 * ends - 2)

    stage1 = []
    stage2 = []
    stage3 = []

    def exchange(n, src, dst, scale, gots, sems, peer):
        cs, cr, ss, sr = sems
        return [
            remote(scale[n], gots[n], ss.at[n], sr.at[n], peer),
            remote(src[n], dst[n], cs.at[n], cr.at[n], peer),
        ]

    progress = {"middle": 0, "started": 0}

    def pump():
        while progress["started"] < min(len(stage1), progress["middle"] + WINDOW):
            for copy in stage1[progress["started"]]:
                copy.start()
            progress["started"] += 1

    def middle(n):
        second, first, number = chunks[n]
        for copy in stage1[n]:
            copy.wait_recv()
        for i in range(number):
            base = (first + i) * local
            if n % 2 == 0:
                value = acc[second][base : base + half, :]
            else:
                value = jnp.concatenate(
                    [
                        acc[second][base : base + quarter, :],
                        acc[second][base + half : base + half + quarter, :],
                    ],
                    axis=0,
                )
            value = value + wide(got1[n][i * half : (i + 1) * half, :]) * gots1[n][i : i + 1, :]
            mid[n][i * quarter : (i + 1) * quarter, :] = value[0:quarter]
            code, scale = coded(value[quarter:])
            scale2[n][i : i + 1, :] = scale
            whole2[i * quarter : (i + 1) * quarter, :] = code
        codes2[n][...] = short(whole2[0 : number * quarter, :])
        copies = exchange(
            n,
            codes2,
            got2,
            scale2,
            gots2,
            (cs2, cr2, ss2, sr2),
            y_peer if n % 2 == 0 else x_peer,
        )
        for copy in copies:
            copy.start()
        stage2.append(copies)
        progress["middle"] += 1
        pump()

    for second in order:
        if second == 0:
            own_action(lhs3, part3, 0)
        all_actions(act3, part3, second)
        acc[second][...] += product(lhs3, act3, second)
        for n, (chunk_second, first, number) in enumerate(chunks):
            if chunk_second != second:
                continue
            for i in range(number):
                base = (first + i) * local
                if n % 2 == 0:
                    value = acc[second][base + half : base + local, :]
                else:
                    value = jnp.concatenate(
                        [
                            acc[second][base + quarter : base + half, :],
                            acc[second][base + half + quarter : base + local, :],
                        ],
                        axis=0,
                    )
                code, scale = coded(value)
                codes1[n][i * half : (i + 1) * half, :] = short(code)
                scale1[n][i : i + 1, :] = scale
            stage1.append(
                exchange(
                    n,
                    codes1,
                    got1,
                    scale1,
                    gots1,
                    (cs1, cr1, ss1, sr1),
                    x_peer if n % 2 == 0 else y_peer,
                )
            )
        pump()
        if second == 0:
            for term in order[1:]:
                own_action(lhs3, part3, term)
            hops = spread(0, [x_peer])
        while progress["middle"] < EARLY + second - terms + 1:
            middle(progress["middle"])

    def last(n):
        second, first, number = chunks[n]
        for copy in stage2[n]:
            copy.wait_recv()
        opened = wide(got2[n][...])
        for i in range(number):
            part = slice(i * quarter, (i + 1) * quarter)
            value = mid[n][part, :] + opened[part, :] * gots2[n][i : i + 1, :]
            keep[n][i * own : (i + 1) * own, :] = value[0:own]
            code, scale = coded(value[own:])
            scale3[n][i : i + 1, :] = scale
            for d in range(1, highs):
                whole3[d - 1, i * own : (i + 1) * own, :] = code[(d - 1) * own : d * own]
        copies = []
        for d in range(1, highs):
            codes3[n][d - 1] = short(whole3[d - 1, 0 : number * own, :])
            sem = n * (highs - 1) + d - 1
            copies.append(
                remote(scale3[n], gots3[n].at[d - 1], ss3.at[sem], sr3.at[sem], high_peer(d))
            )
            copies.append(
                remote(
                    codes3[n].at[d - 1], got3[n].at[d - 1], cs3.at[sem], cr3.at[sem], high_peer(d)
                )
            )
        for copy in copies:
            copy.start()
        stage3.append(copies)

    def finish(n, level):
        second, first, number = chunks[n]
        for copy in stage3[n]:
            copy.wait_recv()
        opened = [wide(got3[n][d - 1]) for d in range(1, highs)]
        for i in range(number):
            q = first + i
            value = keep[n][i * own : (i + 1) * own, :]
            for d in range(1, highs):
                value = value + (
                    opened[d - 1][i * own : (i + 1) * own, :] * gots3[n][d - 1, i : i + 1, :]
                )
            factor = 1.0 / (total_cells * jnp.sqrt(level[q : q + 1] * level[second : second + 1]))
            pair = q * terms - q * (q - 1) // 2 + second - q
            out[pair] = value * factor

    level = None
    finished = 0
    for t in range(count + LAG + 4):
        if progress["middle"] <= t < count:
            middle(t)
        if t == 1:
            lvl[1][...] = gathered(0, hops)
            hops = spread(1, [y_peer])
        if 0 <= t - LAG < count:
            last(t - LAG)
        if t == LAG:
            lvl[2][...] = gathered(1, hops)
            hops = spread(2, [high_peer(d) for d in range(1, highs)])
        if t == LAG + 2:
            lvl[3][...] = gathered(2, hops)
            hops = spread(3, [partner])
        if t == LAG + 4:
            lvl[4][...] = gathered(3, hops)
            hops = spread(4, [sibling])
        if t == LAG + 6:
            total = gathered(4, hops)
            level = jnp.sum(total, axis=1, keepdims=True) / (rows * total_cells) + 1e-06
        while t >= LAG + 6 and finished <= t - LAG - 4 and finished < count:
            finish(finished, level)
            finished += 1
    for copies in stage1 + stage2 + stage3:
        sends.extend(copies)
    for copy in sends + across_copies + relays + halos + halo_relays:
        copy.wait_send()


def per_device(basis, slab_region, coef_index, coef_table):
    terms = coef_index.shape[1]
    rows, cells_dev = basis.shape
    slabs_dev = slab_region.shape[0]
    width = cells_dev // slabs_dev
    devices = lax.axis_size("mode")
    highs = devices // 16
    own = rows // devices
    span = slabs_dev * 2
    local = 4 * highs * own
    half, quarter = local // 2, local // 4
    sizes = [number for _, _, number in chunk_list(terms)]
    count = len(sizes)
    tall = terms + -terms % 8
    f32, b16, i16 = jnp.float32, jnp.bfloat16, jnp.int16
    ends = slabs_dev - 2
    depths = [(span - 2) * width, 2 * (ends - 1) * width, (span - 2 * ends + 4) * width]
    dma = pltpu.SemaphoreType.DMA
    vmem = pltpu.VMEM
    scratch = [
        vmem((2 * (span + 2), rows, width), b16),
        vmem((4, tall, width), f32),
        vmem((2 * span, tall, width), f32),
        vmem((2 * (span + 2), local, width), b16),
    ]
    scratch += [vmem((terms * local, k), b16) for k in depths]
    scratch += [vmem((2, rows, k), b16) for k in depths]
    scratch += [vmem((CHUNK * quarter, rows), f32), vmem((highs - 1, CHUNK * own, rows), f32)]
    scratch += [vmem(((q + 1) * local, rows), f32) for q in range(terms)]
    for size in (half, quarter):
        scratch += [vmem((n * size, rows), i16) for n in sizes] * 2
        scratch += [vmem((n, rows), f32) for n in sizes] * 2
    scratch += [vmem((highs - 1, n * own, rows), i16) for n in sizes] * 2
    scratch += [vmem((n, rows), f32) for n in sizes]
    scratch += [vmem((highs - 1, n, rows), f32) for n in sizes]
    scratch += [vmem((n * quarter, rows), f32) for n in sizes]
    scratch += [vmem((n * own, rows), f32) for n in sizes]
    fans = (1, 1, highs - 1, 1, 1)
    scratch += [vmem((tall, width), f32)] * 5
    scratch += [vmem((n, tall, width), f32) for n in fans]
    scratch += [
        pltpu.SMEM(slab_region.shape, jnp.int32),
        pltpu.SMEM(coef_index.shape[::-1], jnp.int32),
        pltpu.SMEM(coef_table.shape, f32),
        pltpu.SemaphoreType.REGULAR((3,)),
        dma((slabs_dev + 3,)),
    ]
    scratch += [dma((slabs_dev,))] * 2
    scratch += [dma((1,))] * 2
    scratch += [dma((slabs_dev,))] * 2
    scratch += [dma((2,))] * 4
    scratch += [dma((3,))] * 2
    scratch += [dma((count,))] * 8
    scratch += [dma((count * (highs - 1),))] * 4
    scratch += [dma((n,)) for n in fans] * 2
    return pl.pallas_call(
        functools.partial(gram_kernel, terms, highs, own, slabs_dev, cells_dev * devices),
        out_shape=jax.ShapeDtypeStruct((terms * (terms + 1) // 2, own, rows), f32),
        in_specs=[pl.BlockSpec(memory_space=pltpu.HBM)] * 4,
        out_specs=pl.BlockSpec(memory_space=pltpu.VMEM),
        scratch_shapes=scratch,
        compiler_params=pltpu.CompilerParams(
            collective_id=0, has_side_effects=True, vmem_limit_bytes=62 << 20
        ),
    )(basis, slab_region, coef_index.T, coef_table)


def solution(mesh):
    return jax.shard_map(
        per_device,
        mesh=mesh,
        in_specs=(P("groups", "mode"), P(("groups", "mode")), P("groups", None), P("groups")),
        out_specs=P(None, ("groups", "mode"), None),
        check_vma=False,
    )
```

```python
import functools

import jax
import jax.numpy as jnp
from jax import lax
from jax.experimental import pallas as pl
from jax.experimental.pallas import tpu as pltpu
from jax.sharding import PartitionSpec as P

CHUNK = 3
WINDOW = 4
EARLY = 0
LAG = 3


def chunk_list(terms):
    chunks = []
    for second in range(terms):
        first = 0
        while first <= second:
            number = -(-(second + 1 - first) // -(-(second + 1 - first) // CHUNK))
            chunks.append((second, first, number))
            first += number
    return chunks


def one_action(term, here, before, after, across, opposite, kappa):
    value = here.astype(jnp.float32)
    if term == 0:
        stencil = 2.0 * value - before.astype(jnp.float32) - after.astype(jnp.float32)
    elif term == 1:
        stencil = jnp.dot(here, across, preferred_element_type=jnp.float32)
    elif term == 2:
        stencil = value - before.astype(jnp.float32)
    elif term == 3:
        stencil = value - after.astype(jnp.float32)
    elif term == 4:
        stencil = jnp.dot(here, opposite, preferred_element_type=jnp.float32)
    else:
        stencil = value
    return (kappa * stencil).astype(jnp.bfloat16)


def coded(value, floor=1e-30):
    peak = jnp.maximum(jnp.max(jnp.abs(value), axis=0, keepdims=True), floor)
    return jnp.round(value * (32000.0 / peak)), peak * (1.0 / 32000.0)


def short(code):
    return code.astype(jnp.int32).astype(jnp.int16)


def wide(code):
    return code.astype(jnp.int32).astype(jnp.float32)


def gram_kernel(terms, highs, own, slabs_dev, total_cells, *refs):
    basis, region_in, index_in, table_in, out = refs[:5]
    chunks = chunk_list(terms)
    count = len(chunks)
    field, packed, weights, mine, lhs1, lhs2, lhs3, act1, act2, act3, whole2, whole3 = refs[5:17]
    at = 17
    acc = refs[at : at + terms]
    at += terms
    buffers = []
    for _ in range(14):
        buffers.append(refs[at : at + count])
        at += count
    (codes1, got1, scale1, gots1, codes2, got2, scale2, gots2) = buffers[:8]
    (codes3, got3, scale3, gots3, mid, keep) = buffers[8:]
    lvl = refs[at : at + 5]
    lvl_in = refs[at + 5 : at + 10]
    region, index, table, heard = refs[at + 10 : at + 14]
    at += 14
    (load_sem, xs, xr, sib_s, sib_r, rel_s, rel_r, hs, hr, hrel_s, hrel_r, ks, kr) = refs[at : at + 13]
    at += 13
    (cs1, cr1, ss1, sr1, cs2, cr2, ss2, sr2, cs3, cr3, ss3, sr3) = refs[at : at + 12]
    lvl_s = refs[at + 12 : at + 17]
    lvl_r = refs[at + 17 : at + 22]

    rows, width = field.shape[1], field.shape[2]
    entries = table_in.shape[0]
    span = 2 * slabs_dev
    stride = span + 2
    chips = 8 * highs
    local = 4 * highs * own
    half = local // 2
    quarter = local // 4
    me = lax.axis_index("mode")
    chip = me // 2
    core = me % 2
    x = chip % 2
    y = (chip // 2) % 2
    level_z = chip // 4
    low = level_z % 2
    high = level_z // 2

    def across_pair(c):
        return c + 4 - 8 * ((c // 4) % 2)

    def device(c):
        return c * 2 + core

    other = across_pair(chip)
    step = 2 * core - 1
    ahead = lax.rem(chip + chips + step, chips)
    other_next = lax.rem(other + chips + step, chips)
    sibling = chip * 2 + 1 - core
    partner = device(other)
    x_peer = device(chip + 1 - 2 * x)
    y_peer = device(chip + 2 - 4 * y)

    def high_peer(d):
        return device(chip + 8 * (lax.rem(high + d, highs) - high))

    def remote(src, dst, send, recv, peer):
        return pltpu.make_async_remote_copy(
            src_ref=src,
            dst_ref=dst,
            send_sem=send,
            recv_sem=recv,
            device_id={"mode": peer},
            device_id_type=pl.DeviceIdType.MESH,
        )

    first_slot = 1 + core * slabs_dev
    loads = [
        pltpu.make_async_copy(
            basis.at[:, pl.ds(s * width, width)], field.at[first_slot + s], load_sem.at[s]
        )
        for s in range(slabs_dev)
    ]
    scalars = [
        pltpu.make_async_copy(src, dst, load_sem.at[slabs_dev + n])
        for n, (src, dst) in enumerate(((region_in, region), (index_in, index), (table_in, table)))
    ]
    for copy in scalars + loads:
        copy.start()

    barrier = pltpu.get_barrier_semaphore()
    linked = [partner, x_peer, y_peer] + [high_peer(d) for d in range(1, highs)]

    def signal(semaphore, peer):
        pl.semaphore_signal(
            semaphore, inc=1, device_id={"mode": peer}, device_id_type=pl.DeviceIdType.MESH
        )

    for peer in linked + [sibling]:
        signal(barrier, peer)
    for copy in scalars:
        copy.wait()

    tall = weights.shape[1]
    piece = width // slabs_dev
    row_at = lax.broadcasted_iota(jnp.int32, (tall, width), 0)
    lane_at = lax.broadcasted_iota(jnp.int32, (tall, width), 1)
    value = jnp.zeros((tall, width), jnp.float32)
    for s in range(slabs_dev):
        where = region[s]
        lanes = (lane_at >= s * piece) & (lane_at < (s + 1) * piece)
        for term in range(terms):
            entry = index[term, where]
            kappa = jnp.where(entry < entries, table[jnp.minimum(entry, entries - 1)], 0.0)
            value = jnp.where(lanes & (row_at == term), kappa, value)
    packed[core] = value

    wi = lax.broadcasted_iota(jnp.int32, (width, width), 0)
    wj = lax.broadcasted_iota(jnp.int32, (width, width), 1)
    beside_one = jnp.where((wi == wj + 1) | (wj == wi + 1), 1.0, 0.0)
    same = jnp.where(wi == wj, 1.0, 0.0)
    flip = jnp.where(wi + wj == width - 1, 1.0, 0.0)
    across = (2.0 * same - beside_one).astype(jnp.bfloat16)
    opposite = (same - flip).astype(jnp.bfloat16)
    ri = lax.broadcasted_iota(jnp.int32, (local, rows), 0)
    rj = lax.broadcasted_iota(jnp.int32, (local, rows), 1)
    source = ri
    for dx in range(2):
        for dy in range(2):
            for dh in range(highs):
                place = (dx * 2 + dy) * highs + dh
                home_z = lax.rem(high + dh, highs) * 2 + low
                home_y = y + dy - 2 * y * dy
                home_x = x + dx - 2 * x * dx
                home = ((home_z * 2 + home_y) * 2 + home_x) * 2 + core
                source = jnp.where(ri >= place * own, ri + (home * own - place * own), source)
    select = jnp.where(rj == source, 1.0, 0.0).astype(jnp.bfloat16)

    pl.semaphore_wait(barrier, len(linked) + 1)
    for copy in loads:
        copy.wait()

    def turn(k):
        return k + core * (slabs_dev - 1 - 2 * k)

    across_copies = []
    relays = []
    for k in range(slabs_dev):
        slot = first_slot + turn(k)
        across_copies.append(
            remote(field.at[slot], field.at[stride + slot], xs.at[k], xr.at[k], partner)
        )
        slot = stride + slot
        relays.append(remote(field.at[slot], field.at[slot], rel_s.at[k], rel_r.at[k], sibling))
    block = pl.ds(first_slot, slabs_dev)
    beside = remote(field.at[block], field.at[block], sib_s.at[0], sib_r.at[0], sibling)
    edge = 1 + core * (span - 1)
    beyond = (1 - core) * (span + 1)
    halos = []
    halo_relays = []
    arrivals = []
    for n, (origin, toward) in enumerate(((chip, ahead), (other, other_next))):
        inside = jnp.where((toward // 4) == (origin // 4) + 1 - 2 * ((origin // 4) % 2), 1, 0)
        landing = n + inside - 2 * n * inside
        target = toward + landing * (across_pair(toward) - toward)
        halos.append(
            remote(
                field.at[n * stride + edge],
                field.at[landing * stride + beyond],
                hs.at[n],
                hr.at[landing],
                device(target),
            )
        )
        slot = n * stride + beyond
        arrivals.append(remote(field.at[slot], field.at[slot], hs.at[n], hr.at[n], partner))
        halo_relays.append(
            remote(field.at[slot], field.at[slot], hrel_s.at[n], hrel_r.at[n], sibling)
        )
    small = [
        remote(packed.at[core], packed.at[core + shift], ks.at[n], kr.at[n], peer)
        for n, (peer, shift) in enumerate(((sibling, 0), (partner, 2)))
    ]
    small.append(remote(packed.at[2 + core], packed.at[2 + core], ks.at[2], kr.at[2], sibling))
    for copy in small[:2] + across_copies[:1] + [beside] + across_copies[1:-1]:
        copy.start()

    def tell(n):
        for peer in linked:
            signal(heard.at[n], peer)

    def hear(n):
        pl.semaphore_wait(heard.at[n], len(linked))

    tell(0)

    def pick(first, number):
        for s in range(number):
            mine[first + s] = jnp.dot(
                select, field[first + s], preferred_element_type=jnp.float32
            ).astype(jnp.bfloat16)

    def acted(term, source_ref, spot):
        part, slab = spot
        alone = term in (1, 4, 5)
        slot = part * stride + 1 + slab
        return one_action(
            term,
            source_ref[slot],
            None if alone else source_ref[slot - 1],
            None if alone else source_ref[slot + 1],
            across,
            opposite,
            weights[part * span + slab, term : term + 1, :],
        )

    lvl[0][...] = jnp.zeros_like(lvl[0])

    def own_action(lhs, part, term):
        squares = None
        for s, spot in enumerate(part):
            value = acted(term, mine, spot)
            lhs[term * local : (term + 1) * local, s * width : (s + 1) * width] = value
            value = value.astype(jnp.float32)
            squares = value * value if squares is None else squares + value * value
        lvl[0][term : term + 1, :] += jnp.sum(squares, axis=0, keepdims=True)

    def all_actions(act, part, second):
        for s, spot in enumerate(part):
            act[second % 2, :, s * width : (s + 1) * width] = acted(second, field, spot)

    def product(lhs, act, second):
        return lax.dot_general(
            lhs[0 : (second + 1) * local, :],
            act[second % 2],
            (((1,), (1,)), ((), ())),
            preferred_element_type=jnp.float32,
        )

    sends = []

    def spread(n, peers):
        copies = [
            remote(lvl[n], lvl_in[n].at[d], lvl_s[n].at[d], lvl_r[n].at[d], peer)
            for d, peer in enumerate(peers)
        ]
        for copy in copies:
            copy.start()
        sends.extend(copies)
        return copies

    def gathered(n, copies):
        for copy in copies:
            copy.wait_recv()
        total = lvl[n][...]
        for d in range(len(copies)):
            total = total + lvl_in[n][d]
        return total

    ends = slabs_dev - 2
    part1 = [(0, s) for s in range(1, span - 1)]
    part2 = [(1, s) for s in range(1, span - 1) if s < ends or s >= span - ends]
    part3 = [(1, s) for s in range(ends, span - ends)]
    part3 += [(n, s) for n in range(2) for s in (0, span - 1)]
    order = list(range(terms))

    def expand(first):
        for n in range(first, first + 2):
            source_value = packed[n]
            for s in range(slabs_dev):
                lanes = (lane_at >= s * piece) & (lane_at < (s + 1) * piece)
                value = jnp.where(lanes, source_value, 0.0)
                shift = piece
                while shift < width:
                    value = value + pltpu.roll(value, shift, 1)
                    shift *= 2
                weights[n * slabs_dev + s] = value

    def pass_on(k):
        across_copies[k].wait_recv()
        relays[k].start()

    small[0].wait()
    expand(0)
    hear(0)
    tell(1)
    beside.wait()
    pick(1, span)
    hear(1)
    tell(2)
    small[1].wait()
    small[2].start()
    hear(2)
    halos[0].start()
    pass_on(0)
    halos[1].start()
    across_copies[slabs_dev - 1].start()
    for second in order:
        own_action(lhs1, part1, second)
        all_actions(act1, part1, second)
        acc[second][...] = product(lhs1, act1, second)
        if second == 2:
            pass_on(1)
    small[2].wait()
    expand(2)
    pass_on(2)
    for n in range(2):
        arrivals[n].wait_recv()
        halo_relays[n].start()
    for copy in relays[: slabs_dev - 1]:
        copy.wait_recv()
    pick(stride + 1, ends + 1)
    pick(stride + span - ends, ends + 1)
    for second in order:
        own_action(lhs2, part2, second)
        all_actions(act2, part2, second)
        acc[second][...] += product(lhs2, act2, second)
        if second == 2:
            pass_on(slabs_dev - 1)
    for copy in halo_relays:
        copy.wait_recv()
    for n in range(2):
        pick(n * stride, 1)
        pick(n * stride + span + 1, 1)
    relays[slabs_dev - 1].wait_recv()
    pick(stride + ends + 2, span - 2 * ends - 2)

    stage1 = []
    stage2 = []
    stage3 = []

    def exchange(n, src, dst, scale, gots, sems, peer):
        cs, cr, ss, sr = sems
        return [
            remote(scale[n], gots[n], ss.at[n], sr.at[n], peer),
            remote(src[n], dst[n], cs.at[n], cr.at[n], peer),
        ]

    progress = {"middle": 0, "started": 0}

    def pump():
        while progress["started"] < min(len(stage1), progress["middle"] + WINDOW):
            for copy in stage1[progress["started"]]:
                copy.start()
            progress["started"] += 1

    def middle(n):
        second, first, number = chunks[n]
        for copy in stage1[n]:
            copy.wait_recv()
        for i in range(number):
            base = (first + i) * local
            if n % 2 == 0:
                value = acc[second][base : base + half, :]
            else:
                value = jnp.concatenate(
                    [
                        acc[second][base : base + quarter, :],
                        acc[second][base + half : base + half + quarter, :],
                    ],
                    axis=0,
                )
            value = value + wide(got1[n][i * half : (i + 1) * half, :]) * gots1[n][i : i + 1, :]
            mid[n][i * quarter : (i + 1) * quarter, :] = value[0:quarter]
            code, scale = coded(value[quarter:])
            scale2[n][i : i + 1, :] = scale
            whole2[i * quarter : (i + 1) * quarter, :] = code
        codes2[n][...] = short(whole2[0 : number * quarter, :])
        copies = exchange(
            n,
            codes2,
            got2,
            scale2,
            gots2,
            (cs2, cr2, ss2, sr2),
            y_peer if n % 2 == 0 else x_peer,
        )
        for copy in copies:
            copy.start()
        stage2.append(copies)
        progress["middle"] += 1
        pump()

    for second in order:
        if second == 0:
            own_action(lhs3, part3, 0)
        all_actions(act3, part3, second)
        acc[second][...] += product(lhs3, act3, second)
        for n, (chunk_second, first, number) in enumerate(chunks):
            if chunk_second != second:
                continue
            for i in range(number):
                base = (first + i) * local
                if n % 2 == 0:
                    value = acc[second][base + half : base + local, :]
                else:
                    value = jnp.concatenate(
                        [
                            acc[second][base + quarter : base + half, :],
                            acc[second][base + half + quarter : base + local, :],
                        ],
                        axis=0,
                    )
                code, scale = coded(value)
                codes1[n][i * half : (i + 1) * half, :] = short(code)
                scale1[n][i : i + 1, :] = scale
            stage1.append(
                exchange(
                    n,
                    codes1,
                    got1,
                    scale1,
                    gots1,
                    (cs1, cr1, ss1, sr1),
                    x_peer if n % 2 == 0 else y_peer,
                )
            )
        pump()
        if second == 0:
            for term in order[1:]:
                own_action(lhs3, part3, term)
            hops = spread(0, [x_peer])
        while progress["middle"] < EARLY + second - terms + 1:
            middle(progress["middle"])

    def last(n):
        second, first, number = chunks[n]
        for copy in stage2[n]:
            copy.wait_recv()
        opened = wide(got2[n][...])
        for i in range(number):
            part = slice(i * quarter, (i + 1) * quarter)
            value = mid[n][part, :] + opened[part, :] * gots2[n][i : i + 1, :]
            keep[n][i * own : (i + 1) * own, :] = value[0:own]
            code, scale = coded(value[own:])
            scale3[n][i : i + 1, :] = scale
            for d in range(1, highs):
                whole3[d - 1, i * own : (i + 1) * own, :] = code[(d - 1) * own : d * own]
        copies = []
        for d in range(1, highs):
            codes3[n][d - 1] = short(whole3[d - 1, 0 : number * own, :])
            sem = n * (highs - 1) + d - 1
            copies.append(
                remote(scale3[n], gots3[n].at[d - 1], ss3.at[sem], sr3.at[sem], high_peer(d))
            )
            copies.append(
                remote(
                    codes3[n].at[d - 1], got3[n].at[d - 1], cs3.at[sem], cr3.at[sem], high_peer(d)
                )
            )
        for copy in copies:
            copy.start()
        stage3.append(copies)

    def finish(n, level):
        second, first, number = chunks[n]
        for copy in stage3[n]:
            copy.wait_recv()
        opened = [wide(got3[n][d - 1]) for d in range(1, highs)]
        for i in range(number):
            q = first + i
            value = keep[n][i * own : (i + 1) * own, :]
            for d in range(1, highs):
                value = value + (
                    opened[d - 1][i * own : (i + 1) * own, :] * gots3[n][d - 1, i : i + 1, :]
                )
            factor = 1.0 / (total_cells * jnp.sqrt(level[q : q + 1] * level[second : second + 1]))
            pair = q * terms - q * (q - 1) // 2 + second - q
            out[pair] = value * factor

    level = None
    finished = 0
    for t in range(count + LAG + 4):
        if progress["middle"] <= t < count:
            middle(t)
        if t == 1:
            lvl[1][...] = gathered(0, hops)
            hops = spread(1, [y_peer])
        if 0 <= t - LAG < count:
            last(t - LAG)
        if t == LAG:
            lvl[2][...] = gathered(1, hops)
            hops = spread(2, [high_peer(d) for d in range(1, highs)])
        if t == LAG + 2:
            lvl[3][...] = gathered(2, hops)
            hops = spread(3, [partner])
        if t == LAG + 4:
            lvl[4][...] = gathered(3, hops)
            hops = spread(4, [sibling])
        if t == LAG + 6:
            total = gathered(4, hops)
            level = jnp.sum(total, axis=1, keepdims=True) / (rows * total_cells) + 1e-06
        while t >= LAG + 6 and finished <= t - LAG - 4 and finished < count:
            finish(finished, level)
            finished += 1
    for copies in stage1 + stage2 + stage3:
        sends.extend(copies)
    for copy in sends + across_copies + relays + halos + halo_relays:
        copy.wait_send()


def per_device(basis, slab_region, coef_index, coef_table):
    terms = coef_index.shape[1]
    rows, cells_dev = basis.shape
    slabs_dev = slab_region.shape[0]
    width = cells_dev // slabs_dev
    devices = lax.axis_size("mode")
    highs = devices // 16
    own = rows // devices
    span = slabs_dev * 2
    local = 4 * highs * own
    half, quarter = local // 2, local // 4
    sizes = [number for _, _, number in chunk_list(terms)]
    count = len(sizes)
    tall = terms + -terms % 8
    f32, b16, i16 = jnp.float32, jnp.bfloat16, jnp.int16
    ends = slabs_dev - 2
    depths = [(span - 2) * width, 2 * (ends - 1) * width, (span - 2 * ends + 4) * width]
    dma = pltpu.SemaphoreType.DMA
    vmem = pltpu.VMEM
    scratch = [
        vmem((2 * (span + 2), rows, width), b16),
        vmem((4, tall, width), f32),
        vmem((2 * span, tall, width), f32),
        vmem((2 * (span + 2), local, width), b16),
    ]
    scratch += [vmem((terms * local, k), b16) for k in depths]
    scratch += [vmem((2, rows, k), b16) for k in depths]
    scratch += [vmem((CHUNK * quarter, rows), f32), vmem((highs - 1, CHUNK * own, rows), f32)]
    scratch += [vmem(((q + 1) * local, rows), f32) for q in range(terms)]
    for size in (half, quarter):
        scratch += [vmem((n * size, rows), i16) for n in sizes] * 2
        scratch += [vmem((n, rows), f32) for n in sizes] * 2
    scratch += [vmem((highs - 1, n * own, rows), i16) for n in sizes] * 2
    scratch += [vmem((n, rows), f32) for n in sizes]
    scratch += [vmem((highs - 1, n, rows), f32) for n in sizes]
    scratch += [vmem((n * quarter, rows), f32) for n in sizes]
    scratch += [vmem((n * own, rows), f32) for n in sizes]
    fans = (1, 1, highs - 1, 1, 1)
    scratch += [vmem((tall, width), f32)] * 5
    scratch += [vmem((n, tall, width), f32) for n in fans]
    scratch += [
        pltpu.SMEM(slab_region.shape, jnp.int32),
        pltpu.SMEM(coef_index.shape[::-1], jnp.int32),
        pltpu.SMEM(coef_table.shape, f32),
        pltpu.SemaphoreType.REGULAR((3,)),
        dma((slabs_dev + 3,)),
    ]
    scratch += [dma((slabs_dev,))] * 2
    scratch += [dma((1,))] * 2
    scratch += [dma((slabs_dev,))] * 2
    scratch += [dma((2,))] * 4
    scratch += [dma((3,))] * 2
    scratch += [dma((count,))] * 8
    scratch += [dma((count * (highs - 1),))] * 4
    scratch += [dma((n,)) for n in fans] * 2
    return pl.pallas_call(
        functools.partial(gram_kernel, terms, highs, own, slabs_dev, cells_dev * devices),
        out_shape=jax.ShapeDtypeStruct((terms * (terms + 1) // 2, own, rows), f32),
        in_specs=[pl.BlockSpec(memory_space=pltpu.HBM)] * 4,
        out_specs=pl.BlockSpec(memory_space=pltpu.VMEM),
        scratch_shapes=scratch,
        compiler_params=pltpu.CompilerParams(
            collective_id=0, has_side_effects=True, vmem_limit_bytes=40 << 20
        ),
    )(
        pltpu.with_memory_space_constraint(basis, pltpu.HBM),
        pltpu.with_memory_space_constraint(slab_region, pltpu.HBM),
        pltpu.with_memory_space_constraint(coef_index.T, pltpu.HBM),
        pltpu.with_memory_space_constraint(coef_table, pltpu.HBM),
    )


def solution(mesh):
    return jax.shard_map(
        per_device,
        mesh=mesh,
        in_specs=(P("groups", "mode"), P(("groups", "mode")), P("groups", None), P("groups")),
        out_specs=P(None, ("groups", "mode"), None),
        check_vma=False,
    )
```

```python
import functools

import jax
import jax.numpy as jnp
from jax import lax
from jax.experimental import pallas as pl
from jax.experimental.pallas import tpu as pltpu
from jax.sharding import PartitionSpec as P

CHUNK = 3
WINDOW = 4
EARLY = 0
LAG = 3


def chunk_list(terms):
    chunks = []
    for second in range(terms):
        first = 0
        while first <= second:
            number = -(-(second + 1 - first) // -(-(second + 1 - first) // CHUNK))
            chunks.append((second, first, number))
            first += number
    return chunks


def one_action(term, here, before, after, across, opposite, kappa):
    value = here.astype(jnp.float32)
    if term == 0:
        stencil = 2.0 * value - before.astype(jnp.float32) - after.astype(jnp.float32)
    elif term == 1:
        stencil = jnp.dot(here, across, preferred_element_type=jnp.float32)
    elif term == 2:
        stencil = value - before.astype(jnp.float32)
    elif term == 3:
        stencil = value - after.astype(jnp.float32)
    elif term == 4:
        stencil = jnp.dot(here, opposite, preferred_element_type=jnp.float32)
    else:
        stencil = value
    return (kappa * stencil).astype(jnp.bfloat16)


def coded(value, floor=1e-30):
    peak = jnp.maximum(jnp.max(jnp.abs(value), axis=0, keepdims=True), floor)
    return jnp.round(value * (32000.0 / peak)), peak * (1.0 / 32000.0)


def short(code):
    return code.astype(jnp.int32).astype(jnp.int16)


def wide(code):
    return code.astype(jnp.int32).astype(jnp.float32)


def gram_kernel(terms, highs, own, slabs_dev, total_cells, *refs):
    basis, region_in, index_in, table_in, out = refs[:5]
    chunks = chunk_list(terms)
    count = len(chunks)
    field, packed, weights, mine, lhs1, lhs2, lhs3, act1, act2, act3, whole2, whole3 = refs[5:17]
    at = 17
    acc = refs[at : at + terms]
    at += terms
    buffers = []
    for _ in range(14):
        buffers.append(refs[at : at + count])
        at += count
    (codes1, got1, scale1, gots1, codes2, got2, scale2, gots2) = buffers[:8]
    (codes3, got3, scale3, gots3, mid, keep) = buffers[8:]
    lvl = refs[at : at + 5]
    lvl_in = refs[at + 5 : at + 10]
    region, index, table, heard = refs[at + 10 : at + 14]
    at += 14
    (load_sem, xs, xr, sib_s, sib_r, rel_s, rel_r, hs, hr, hrel_s, hrel_r, ks, kr) = refs[at : at + 13]
    at += 13
    (cs1, cr1, ss1, sr1, cs2, cr2, ss2, sr2, cs3, cr3, ss3, sr3) = refs[at : at + 12]
    lvl_s = refs[at + 12 : at + 17]
    lvl_r = refs[at + 17 : at + 22]

    rows, width = field.shape[1], field.shape[2]
    entries = table_in.shape[0]
    span = 2 * slabs_dev
    stride = span + 2
    chips = 8 * highs
    local = 4 * highs * own
    half = local // 2
    quarter = local // 4
    me = lax.axis_index("mode")
    chip = me // 2
    core = me % 2
    x = chip % 2
    y = (chip // 2) % 2
    level_z = chip // 4
    low = level_z % 2
    high = level_z // 2

    def across_pair(c):
        return c + 4 - 8 * ((c // 4) % 2)

    def device(c):
        return c * 2 + core

    other = across_pair(chip)
    step = 2 * core - 1
    ahead = lax.rem(chip + chips + step, chips)
    other_next = lax.rem(other + chips + step, chips)
    sibling = chip * 2 + 1 - core
    partner = device(other)
    x_peer = device(chip + 1 - 2 * x)
    y_peer = device(chip + 2 - 4 * y)

    def high_peer(d):
        return device(chip + 8 * (lax.rem(high + d, highs) - high))

    def remote(src, dst, send, recv, peer):
        return pltpu.make_async_remote_copy(
            src_ref=src,
            dst_ref=dst,
            send_sem=send,
            recv_sem=recv,
            device_id={"mode": peer},
            device_id_type=pl.DeviceIdType.MESH,
        )

    first_slot = 1 + core * slabs_dev
    loads = [
        pltpu.make_async_copy(
            basis.at[:, pl.ds(s * width, width)], field.at[first_slot + s], load_sem.at[s]
        )
        for s in range(slabs_dev)
    ]
    scalars = [
        pltpu.make_async_copy(src, dst, load_sem.at[slabs_dev + n])
        for n, (src, dst) in enumerate(((region_in, region), (index_in, index), (table_in, table)))
    ]
    for copy in scalars + loads:
        copy.start()

    barrier = pltpu.get_barrier_semaphore()
    linked = [partner, x_peer, y_peer] + [high_peer(d) for d in range(1, highs)]

    def signal(semaphore, peer):
        pl.semaphore_signal(
            semaphore, inc=1, device_id={"mode": peer}, device_id_type=pl.DeviceIdType.MESH
        )

    for peer in linked + [sibling]:
        signal(barrier, peer)
    for copy in scalars:
        copy.wait()

    tall = weights.shape[1]
    piece = width // slabs_dev
    row_at = lax.broadcasted_iota(jnp.int32, (tall, width), 0)
    lane_at = lax.broadcasted_iota(jnp.int32, (tall, width), 1)
    value = jnp.zeros((tall, width), jnp.float32)
    for s in range(slabs_dev):
        where = region[s]
        lanes = (lane_at >= s * piece) & (lane_at < (s + 1) * piece)
        for term in range(terms):
            entry = index[term, where]
            kappa = jnp.where(entry < entries, table[jnp.minimum(entry, entries - 1)], 0.0)
            value = jnp.where(lanes & (row_at == term), kappa, value)
    packed[core] = value

    wi = lax.broadcasted_iota(jnp.int32, (width, width), 0)
    wj = lax.broadcasted_iota(jnp.int32, (width, width), 1)
    beside_one = jnp.where((wi == wj + 1) | (wj == wi + 1), 1.0, 0.0)
    same = jnp.where(wi == wj, 1.0, 0.0)
    flip = jnp.where(wi + wj == width - 1, 1.0, 0.0)
    across = (2.0 * same - beside_one).astype(jnp.bfloat16)
    opposite = (same - flip).astype(jnp.bfloat16)
    ri = lax.broadcasted_iota(jnp.int32, (local, rows), 0)
    rj = lax.broadcasted_iota(jnp.int32, (local, rows), 1)
    source = ri
    for dx in range(2):
        for dy in range(2):
            for dh in range(highs):
                place = (dx * 2 + dy) * highs + dh
                home_z = lax.rem(high + dh, highs) * 2 + low
                home_y = y + dy - 2 * y * dy
                home_x = x + dx - 2 * x * dx
                home = ((home_z * 2 + home_y) * 2 + home_x) * 2 + core
                source = jnp.where(ri >= place * own, ri + (home * own - place * own), source)
    select = jnp.where(rj == source, 1.0, 0.0).astype(jnp.bfloat16)

    pl.semaphore_wait(barrier, len(linked) + 1)
    for copy in loads:
        copy.wait()

    def turn(k):
        return k + core * (slabs_dev - 1 - 2 * k)

    across_copies = []
    relays = []
    for k in range(slabs_dev):
        slot = first_slot + turn(k)
        across_copies.append(
            remote(field.at[slot], field.at[stride + slot], xs.at[k], xr.at[k], partner)
        )
        slot = stride + slot
        relays.append(remote(field.at[slot], field.at[slot], rel_s.at[k], rel_r.at[k], sibling))
    block = pl.ds(first_slot, slabs_dev)
    beside = remote(field.at[block], field.at[block], sib_s.at[0], sib_r.at[0], sibling)
    edge = 1 + core * (span - 1)
    beyond = (1 - core) * (span + 1)
    halos = []
    halo_relays = []
    arrivals = []
    for n, (origin, toward) in enumerate(((chip, ahead), (other, other_next))):
        inside = jnp.where((toward // 4) == (origin // 4) + 1 - 2 * ((origin // 4) % 2), 1, 0)
        landing = n + inside - 2 * n * inside
        target = toward + landing * (across_pair(toward) - toward)
        halos.append(
            remote(
                field.at[n * stride + edge],
                field.at[landing * stride + beyond],
                hs.at[n],
                hr.at[landing],
                device(target),
            )
        )
        slot = n * stride + beyond
        arrivals.append(remote(field.at[slot], field.at[slot], hs.at[n], hr.at[n], partner))
        halo_relays.append(
            remote(field.at[slot], field.at[slot], hrel_s.at[n], hrel_r.at[n], sibling)
        )
    small = [
        remote(packed.at[core], packed.at[core + shift], ks.at[n], kr.at[n], peer)
        for n, (peer, shift) in enumerate(((sibling, 0), (partner, 2)))
    ]
    small.append(remote(packed.at[2 + core], packed.at[2 + core], ks.at[2], kr.at[2], sibling))
    for copy in small[:2] + across_copies[:1] + [beside] + across_copies[1:-1]:
        copy.start()

    def tell(n):
        for peer in linked:
            signal(heard.at[n], peer)

    def hear(n):
        pl.semaphore_wait(heard.at[n], len(linked))

    tell(0)

    def pick(first, number):
        for s in range(number):
            mine[first + s] = jnp.dot(
                select, field[first + s], preferred_element_type=jnp.float32
            ).astype(jnp.bfloat16)

    def acted(term, source_ref, spot):
        part, slab = spot
        alone = term in (1, 4, 5)
        slot = part * stride + 1 + slab
        return one_action(
            term,
            source_ref[slot],
            None if alone else source_ref[slot - 1],
            None if alone else source_ref[slot + 1],
            across,
            opposite,
            weights[part * span + slab, term : term + 1, :],
        )

    lvl[0][...] = jnp.zeros_like(lvl[0])

    def own_action(lhs, part, term):
        squares = None
        for s, spot in enumerate(part):
            value = acted(term, mine, spot)
            lhs[term * local : (term + 1) * local, s * width : (s + 1) * width] = value
            value = value.astype(jnp.float32)
            squares = value * value if squares is None else squares + value * value
        lvl[0][term : term + 1, :] += jnp.sum(squares, axis=0, keepdims=True)

    def all_actions(act, part, second):
        for s, spot in enumerate(part):
            act[second % 2, :, s * width : (s + 1) * width] = acted(second, field, spot)

    def product(lhs, act, second):
        return lax.dot_general(
            lhs[0 : (second + 1) * local, :],
            act[second % 2],
            (((1,), (1,)), ((), ())),
            preferred_element_type=jnp.float32,
        )

    sends = []

    def spread(n, peers):
        copies = [
            remote(lvl[n], lvl_in[n].at[d], lvl_s[n].at[d], lvl_r[n].at[d], peer)
            for d, peer in enumerate(peers)
        ]
        for copy in copies:
            copy.start()
        sends.extend(copies)
        return copies

    def gathered(n, copies):
        for copy in copies:
            copy.wait_recv()
        total = lvl[n][...]
        for d in range(len(copies)):
            total = total + lvl_in[n][d]
        return total

    ends = slabs_dev - 2
    part1 = [(0, s) for s in range(1, span - 1)]
    part2 = [(1, s) for s in range(1, span - 1) if s < ends or s >= span - ends]
    part3 = [(1, s) for s in range(ends, span - ends)]
    part3 += [(n, s) for n in range(2) for s in (0, span - 1)]
    order = list(range(terms))

    def expand(first):
        for n in range(first, first + 2):
            source_value = packed[n]
            for s in range(slabs_dev):
                lanes = (lane_at >= s * piece) & (lane_at < (s + 1) * piece)
                value = jnp.where(lanes, source_value, 0.0)
                shift = piece
                while shift < width:
                    value = value + pltpu.roll(value, shift, 1)
                    shift *= 2
                weights[n * slabs_dev + s] = value

    def pass_on(k):
        across_copies[k].wait_recv()
        relays[k].start()

    small[0].wait()
    expand(0)
    hear(0)
    tell(1)
    beside.wait()
    pick(1, span)
    hear(1)
    tell(2)
    small[1].wait()
    small[2].start()
    hear(2)
    halos[0].start()
    pass_on(0)
    halos[1].start()
    across_copies[slabs_dev - 1].start()
    for second in order:
        own_action(lhs1, part1, second)
        all_actions(act1, part1, second)
        acc[second][...] = product(lhs1, act1, second)
        if second == 2:
            pass_on(1)
    small[2].wait()
    expand(2)
    pass_on(2)
    for n in range(2):
        arrivals[n].wait_recv()
        halo_relays[n].start()
    for copy in relays[: slabs_dev - 1]:
        copy.wait_recv()
    pick(stride + 1, ends + 1)
    pick(stride + span - ends, ends + 1)
    for second in order:
        own_action(lhs2, part2, second)
        all_actions(act2, part2, second)
        acc[second][...] += product(lhs2, act2, second)
        if second == 2:
            pass_on(slabs_dev - 1)
    for copy in halo_relays:
        copy.wait_recv()
    for n in range(2):
        pick(n * stride, 1)
        pick(n * stride + span + 1, 1)
    relays[slabs_dev - 1].wait_recv()
    pick(stride + ends + 2, span - 2 * ends - 2)

    stage1 = []
    stage2 = []
    stage3 = []

    def exchange(n, src, dst, scale, gots, sems, peer):
        cs, cr, ss, sr = sems
        return [
            remote(scale[n], gots[n], ss.at[n], sr.at[n], peer),
            remote(src[n], dst[n], cs.at[n], cr.at[n], peer),
        ]

    progress = {"middle": 0, "started": 0}

    def pump():
        while progress["started"] < min(len(stage1), progress["middle"] + WINDOW):
            for copy in stage1[progress["started"]]:
                copy.start()
            progress["started"] += 1

    def middle(n):
        second, first, number = chunks[n]
        for copy in stage1[n]:
            copy.wait_recv()
        for i in range(number):
            base = (first + i) * local
            if n % 2 == 0:
                value = acc[second][base : base + half, :]
            else:
                value = jnp.concatenate(
                    [
                        acc[second][base : base + quarter, :],
                        acc[second][base + half : base + half + quarter, :],
                    ],
                    axis=0,
                )
            value = value + wide(got1[n][i * half : (i + 1) * half, :]) * gots1[n][i : i + 1, :]
            mid[n][i * quarter : (i + 1) * quarter, :] = value[0:quarter]
            code, scale = coded(value[quarter:])
            scale2[n][i : i + 1, :] = scale
            whole2[i * quarter : (i + 1) * quarter, :] = code
        codes2[n][...] = short(whole2[0 : number * quarter, :])
        copies = exchange(
            n,
            codes2,
            got2,
            scale2,
            gots2,
            (cs2, cr2, ss2, sr2),
            y_peer if n % 2 == 0 else x_peer,
        )
        for copy in copies:
            copy.start()
        stage2.append(copies)
        progress["middle"] += 1
        pump()

    for second in order:
        if second < 2:
            own_action(lhs3, part3, second)
        all_actions(act3, part3, second)
        acc[second][...] += product(lhs3, act3, second)
        for n, (chunk_second, first, number) in enumerate(chunks):
            if chunk_second != second:
                continue
            for i in range(number):
                base = (first + i) * local
                if n % 2 == 0:
                    value = acc[second][base + half : base + local, :]
                else:
                    value = jnp.concatenate(
                        [
                            acc[second][base + quarter : base + half, :],
                            acc[second][base + half + quarter : base + local, :],
                        ],
                        axis=0,
                    )
                code, scale = coded(value)
                codes1[n][i * half : (i + 1) * half, :] = short(code)
                scale1[n][i : i + 1, :] = scale
            stage1.append(
                exchange(
                    n,
                    codes1,
                    got1,
                    scale1,
                    gots1,
                    (cs1, cr1, ss1, sr1),
                    x_peer if n % 2 == 0 else y_peer,
                )
            )
        pump()
        if second == 1:
            for term in order[2:]:
                own_action(lhs3, part3, term)
            hops = spread(0, [x_peer])
        while progress["middle"] < EARLY + second - terms + 1:
            middle(progress["middle"])

    def last(n):
        second, first, number = chunks[n]
        for copy in stage2[n]:
            copy.wait_recv()
        opened = wide(got2[n][...])
        for i in range(number):
            part = slice(i * quarter, (i + 1) * quarter)
            value = mid[n][part, :] + opened[part, :] * gots2[n][i : i + 1, :]
            keep[n][i * own : (i + 1) * own, :] = value[0:own]
            code, scale = coded(value[own:])
            scale3[n][i : i + 1, :] = scale
            for d in range(1, highs):
                whole3[d - 1, i * own : (i + 1) * own, :] = code[(d - 1) * own : d * own]
        copies = []
        for d in range(1, highs):
            codes3[n][d - 1] = short(whole3[d - 1, 0 : number * own, :])
            sem = n * (highs - 1) + d - 1
            copies.append(
                remote(scale3[n], gots3[n].at[d - 1], ss3.at[sem], sr3.at[sem], high_peer(d))
            )
            copies.append(
                remote(
                    codes3[n].at[d - 1], got3[n].at[d - 1], cs3.at[sem], cr3.at[sem], high_peer(d)
                )
            )
        for copy in copies:
            copy.start()
        stage3.append(copies)

    def finish(n, level):
        second, first, number = chunks[n]
        for copy in stage3[n]:
            copy.wait_recv()
        opened = [wide(got3[n][d - 1]) for d in range(1, highs)]
        for i in range(number):
            q = first + i
            value = keep[n][i * own : (i + 1) * own, :]
            for d in range(1, highs):
                value = value + (
                    opened[d - 1][i * own : (i + 1) * own, :] * gots3[n][d - 1, i : i + 1, :]
                )
            factor = 1.0 / (total_cells * jnp.sqrt(level[q : q + 1] * level[second : second + 1]))
            pair = q * terms - q * (q - 1) // 2 + second - q
            out[pair] = value * factor

    level = None
    finished = 0
    for t in range(count + LAG + 4):
        if progress["middle"] <= t < count:
            middle(t)
        if t == 1:
            lvl[1][...] = gathered(0, hops)
            hops = spread(1, [y_peer])
        if 0 <= t - LAG < count:
            last(t - LAG)
        if t == LAG:
            lvl[2][...] = gathered(1, hops)
            hops = spread(2, [high_peer(d) for d in range(1, highs)])
        if t == LAG + 2:
            lvl[3][...] = gathered(2, hops)
            hops = spread(3, [partner])
        if t == LAG + 4:
            lvl[4][...] = gathered(3, hops)
            hops = spread(4, [sibling])
        if t == LAG + 6:
            total = gathered(4, hops)
            level = jnp.sum(total, axis=1, keepdims=True) / (rows * total_cells) + 1e-06
        while t >= LAG + 6 and finished <= t - LAG - 4 and finished < count:
            finish(finished, level)
            finished += 1
    for copies in stage1 + stage2 + stage3:
        sends.extend(copies)
    for copy in sends + across_copies + relays + halos + halo_relays:
        copy.wait_send()


def per_device(basis, slab_region, coef_index, coef_table):
    terms = coef_index.shape[1]
    rows, cells_dev = basis.shape
    slabs_dev = slab_region.shape[0]
    width = cells_dev // slabs_dev
    devices = lax.axis_size("mode")
    highs = devices // 16
    own = rows // devices
    span = slabs_dev * 2
    local = 4 * highs * own
    half, quarter = local // 2, local // 4
    sizes = [number for _, _, number in chunk_list(terms)]
    count = len(sizes)
    tall = terms + -terms % 8
    f32, b16, i16 = jnp.float32, jnp.bfloat16, jnp.int16
    ends = slabs_dev - 2
    depths = [(span - 2) * width, 2 * (ends - 1) * width, (span - 2 * ends + 4) * width]
    dma = pltpu.SemaphoreType.DMA
    vmem = pltpu.VMEM
    scratch = [
        vmem((2 * (span + 2), rows, width), b16),
        vmem((4, tall, width), f32),
        vmem((2 * span, tall, width), f32),
        vmem((2 * (span + 2), local, width), b16),
    ]
    scratch += [vmem((terms * local, k), b16) for k in depths]
    scratch += [vmem((2, rows, k), b16) for k in depths]
    scratch += [vmem((CHUNK * quarter, rows), f32), vmem((highs - 1, CHUNK * own, rows), f32)]
    scratch += [vmem(((q + 1) * local, rows), f32) for q in range(terms)]
    for size in (half, quarter):
        scratch += [vmem((n * size, rows), i16) for n in sizes] * 2
        scratch += [vmem((n, rows), f32) for n in sizes] * 2
    scratch += [vmem((highs - 1, n * own, rows), i16) for n in sizes] * 2
    scratch += [vmem((n, rows), f32) for n in sizes]
    scratch += [vmem((highs - 1, n, rows), f32) for n in sizes]
    scratch += [vmem((n * quarter, rows), f32) for n in sizes]
    scratch += [vmem((n * own, rows), f32) for n in sizes]
    fans = (1, 1, highs - 1, 1, 1)
    scratch += [vmem((tall, width), f32)] * 5
    scratch += [vmem((n, tall, width), f32) for n in fans]
    scratch += [
        pltpu.SMEM(slab_region.shape, jnp.int32),
        pltpu.SMEM(coef_index.shape[::-1], jnp.int32),
        pltpu.SMEM(coef_table.shape, f32),
        pltpu.SemaphoreType.REGULAR((3,)),
        dma((slabs_dev + 3,)),
    ]
    scratch += [dma((slabs_dev,))] * 2
    scratch += [dma((1,))] * 2
    scratch += [dma((slabs_dev,))] * 2
    scratch += [dma((2,))] * 4
    scratch += [dma((3,))] * 2
    scratch += [dma((count,))] * 8
    scratch += [dma((count * (highs - 1),))] * 4
    scratch += [dma((n,)) for n in fans] * 2
    return pl.pallas_call(
        functools.partial(gram_kernel, terms, highs, own, slabs_dev, cells_dev * devices),
        out_shape=jax.ShapeDtypeStruct((terms * (terms + 1) // 2, own, rows), f32),
        in_specs=[pl.BlockSpec(memory_space=pltpu.HBM)] * 4,
        out_specs=pl.BlockSpec(memory_space=pltpu.VMEM),
        scratch_shapes=scratch,
        compiler_params=pltpu.CompilerParams(
            collective_id=0, has_side_effects=True, vmem_limit_bytes=40 << 20
        ),
    )(
        pltpu.with_memory_space_constraint(basis, pltpu.HBM),
        pltpu.with_memory_space_constraint(slab_region, pltpu.HBM),
        pltpu.with_memory_space_constraint(coef_index.T, pltpu.HBM),
        pltpu.with_memory_space_constraint(coef_table, pltpu.HBM),
    )


def solution(mesh):
    return jax.shard_map(
        per_device,
        mesh=mesh,
        in_specs=(P("groups", "mode"), P(("groups", "mode")), P("groups", None), P("groups")),
        out_specs=P(None, ("groups", "mode"), None),
        check_vma=False,
    )
```
